512 devices in a mesh: wide: 64 (over z, x), narrow: 8 (over y, core).
Axes of the slice: x: 4, y: 4, z: 16, core: 2. Of those that a mesh axis runs over, the one named last changes fastest.
Arguments:
- features: bfloat16 [32768, 128], P(('wide', 'narrow')), may hold values from -6 to 6
- send_rows: int32 [64, 8, 64, 32], P('wide', 'narrow'), may hold values from 0 to 63
- send_count: int32 [64, 8, 64], P('wide', 'narrow'), may hold values from 1 to 32, as said below
- neighbors: int32 [32768, 16], P(('wide', 'narrow')), may hold values from 0 to 2111, as said below
- w_self: bfloat16 [128, 128], replicated, may hold values from -0.5 to 0.5
- w_neigh: bfloat16 [128, 128], replicated, may hold values from -0.5 to 0.5
- bias_hidden: float32 [128], replicated, may hold values from -4 to 4
- w_out: bfloat16 [128, 256], replicated, may hold values from -0.5 to 0.5
- bias_out: float32 [256], replicated, may hold values from -4 to 4
- tiles: bfloat16 [64, 8, 64, 128, 128], P('wide', 'narrow'), may hold values from 0 to 0.0171875, as said below
- tile_rows: int32 [64, 8, 64], P('wide', 'narrow'), may hold values from 0 to 3
- tile_cols: int32 [64, 8, 64], P('wide', 'narrow'), may hold values from 0 to 31
- tile_count: int32 [64, 8], P('wide', 'narrow'), may hold values from 8 to 64, as said below
- dangling: int32 [32768], P(('wide', 'narrow')), may hold values from 0 to 1, as said below
Outputs:
- propagated: float32 [32768, 256], P(('wide', 'narrow'))
The draws below stay inside these ranges and needn't reach their ends.
Inputs may be any that keep to these rules, and one draw needn't show every extreme that they name: Slots of a boundary row list from send_count on are unused; in every draw some list is full. `neighbors`: an entry below 64 names a row of the node's own device; an entry 64 + p * 32 + c names slot c of the list that device (p, b) keeps for the node's partition, b being the node's narrow index, and c is then below that list's count. Slots from tile_count on are unused; some device uses all 64 slots in every draw. `tile_rows`: tile coordinates of a device may repeat; repeated tiles add. `tiles`: entries are nonnegative. `dangling`: 1 marks a node without out-edges.
All inputs are finite; a program needn't handle non-finite values.
Results may differ from the reference program's by a relative error of at most 0.0003.
Values may be sent and summed in bfloat16 or wider, within the bound.
No kernel may reach another device: no remote copies, remote signals or barrier semaphores. Data moves between devices by JAX's collectives and lax.ppermute only.
A program may use at most 64 MiB of HBM per device.

```python
import jax
import jax.numpy as jnp
from jax import lax

NODE_DEV = 64
F = 128
HID = 128
C = 256
DEG = 16
CAP = 32
TMAX = 64
TILE = 128
ITERS = 3
PARTITIONS = 64
GRID_COLS = 8
NODES = 32768
ROW_TILES = 4
COL_TILES = 32


def boundary_counts(key):
    base = jax.random.fold_in(key, 11)
    first_key, second_key = jax.random.split(base)
    total_lists = PARTITIONS * GRID_COLS * PARTITIONS
    counts = jax.random.randint(first_key, (total_lists,), 1, CAP + 1)
    chosen = jax.random.randint(second_key, (), 0, total_lists)
    counts = counts.at[chosen].set(CAP)
    return counts.reshape(PARTITIONS, GRID_COLS, PARTITIONS).astype(jnp.int32)


def draw_send_count(key, part):
    return boundary_counts(key)


def draw_neighbors(key, part):
    counts = boundary_counts(key)
    keys = jax.random.split(jax.random.fold_in(key, 23), 4)
    layout = (PARTITIONS, GRID_COLS, NODE_DEV * DEG)
    local_rows = jax.random.randint(keys[0], layout, 0, NODE_DEV)
    sources = jax.random.randint(keys[1], layout, 0, PARTITIONS)
    raw_pick = jax.random.randint(keys[2], layout, 0, 1 << 20)
    choose_far = jax.random.randint(keys[3], layout, 0, 2)
    table = jnp.transpose(counts, (2, 1, 0))
    available = jnp.take_along_axis(table, sources, axis=2)
    far_slot = NODE_DEV + sources * CAP + raw_pick % available
    picked = jnp.where(choose_far == 0, local_rows, far_slot)
    return picked.reshape(NODES, DEG).astype(jnp.int32)


def draw_tiles(key, part):
    unit = 0.6 * NODE_DEV / (TMAX * TILE)
    density = 1.0 / TILE
    offsets = jnp.arange(TILE, dtype=jnp.int32)
    spacing = (offsets[None, :] - offsets[:, None]) % TILE
    layout = (GRID_COLS, TMAX, TILE, TILE)

    def one_partition(index):
        inner = jax.random.fold_in(jax.random.fold_in(key, 53), index)
        keys = jax.random.split(inner, 4)
        shifts = jax.random.randint(keys[0], (GRID_COLS, TMAX, 1, 1), 0, TILE)
        on_band = spacing[None, None, :, :] == shifts
        keep = jax.random.uniform(keys[1], layout, dtype=jnp.float32) < density
        band_value = jax.random.uniform(keys[2], layout, dtype=jnp.float32, minval=1.0, maxval=2.0)
        far_value = jax.random.uniform(keys[3], layout, dtype=jnp.float32, minval=0.5, maxval=3.5)
        entry = jnp.where(on_band, band_value, jnp.where(keep, far_value, jnp.zeros((), jnp.float32)))
        return (unit * entry).astype(jnp.bfloat16)
    return lax.map(one_partition, jnp.arange(PARTITIONS))


def draw_tile_count(key, part):
    keys = jax.random.split(jax.random.fold_in(key, 31), 3)
    total_devices = PARTITIONS * GRID_COLS
    lowest = max(TMAX // 8, 1)
    middle = max(TMAX // 3, lowest)
    light = jax.random.randint(keys[0], (total_devices,), lowest, middle + 1)
    heavy = jax.random.randint(keys[1], (total_devices,), 0, 4)
    counts = jnp.where(heavy == 0, TMAX, light)
    chosen = jax.random.randint(keys[2], (), 0, total_devices)
    counts = counts.at[chosen].set(TMAX)
    return counts.reshape(PARTITIONS, GRID_COLS).astype(jnp.int32)


def draw_dangling(key, part):
    draws = jax.random.randint(jax.random.fold_in(key, 41), (PARTITIONS, GRID_COLS * NODE_DEV), 0, 100)
    levels = 10 + 20 * jnp.arange(PARTITIONS, dtype=jnp.int32) // max(PARTITIONS - 1, 1)
    marked = (draws < levels[:, None]).astype(jnp.int32)
    return marked.reshape(NODES)


def set_ends(drawn, stream_key, smallest, top_value):
    longest = drawn.shape.index(max(drawn.shape))
    spots = []
    for shift in (0, 1):
        where = [jax.random.randint(jax.random.fold_in(stream_key, axis), (), 0, length) for axis, length in enumerate(drawn.shape)]
        where[longest] = (where[longest] + shift) % drawn.shape[longest]
        spots.append(tuple(where))
    return drawn.at[spots[0]].set(smallest).at[spots[1]].set(top_value)


def block_levels(key, dims, shards, least, largest):
    level = 1.0
    for axis_at, blocks in shards:
        steps = jax.random.uniform(jax.random.fold_in(jax.random.fold_in(key, 6), axis_at), (blocks,), jnp.float32, least / len(shards), largest / len(shards))
        level = level * jnp.repeat(jnp.exp(steps), dims[axis_at] // blocks).reshape((-1,) + (1,) * (len(dims) - 1 - axis_at))
    return level


def gaussian(rng, shape, scale, limit, cuts=(), kind=jnp.bfloat16):
    array = scale * jax.random.normal(rng, shape, jnp.float32)
    if cuts:
        array = array * block_levels(rng, shape, cuts, -0.22, 0.18)
    return jnp.clip(array, -limit, limit).astype(kind)


def setup_inputs(seed: int = 0) -> dict:
    key_of = jax.random.split(jax.random.key(seed), 15)
    features = gaussian(key_of[0], (NODES, F), 1.0, 6.0, ((0, 512),))
    send_rows = set_ends(jax.random.randint(key_of[1], (PARTITIONS, GRID_COLS, PARTITIONS, CAP), 0, NODE_DEV), jax.random.fold_in(key_of[1], 1), 0, NODE_DEV - 1).astype(jnp.int32)
    send_count = draw_send_count(jax.random.fold_in(key_of[14], 71), 0)
    neighbors = draw_neighbors(jax.random.fold_in(key_of[14], 71), 0)
    w_self = gaussian(key_of[4], (F, HID), F ** -0.5, 0.5)
    w_neigh = gaussian(key_of[5], (F, HID), F ** -0.5, 0.5)
    bias_hidden = gaussian(key_of[6], (HID,), 1.0, 4.0, (), jnp.float32)
    w_out = gaussian(key_of[7], (HID, C), HID ** -0.5, 0.5)
    bias_out = gaussian(key_of[8], (C,), 1.0, 4.0, (), jnp.float32)
    tiles = draw_tiles(jax.random.fold_in(key_of[14], 71), 0)
    tile_rows = set_ends(jax.random.randint(key_of[10], (PARTITIONS, GRID_COLS, TMAX), 0, ROW_TILES), jax.random.fold_in(key_of[10], 1), 0, ROW_TILES - 1).astype(jnp.int32)
    tile_cols = set_ends(jax.random.randint(key_of[11], (PARTITIONS, GRID_COLS, TMAX), 0, COL_TILES), jax.random.fold_in(key_of[11], 1), 0, COL_TILES - 1).astype(jnp.int32)
    tile_count = draw_tile_count(jax.random.fold_in(key_of[14], 71), 0)
    dangling = draw_dangling(jax.random.fold_in(key_of[14], 71), 0)
    return dict(features=features, send_rows=send_rows, send_count=send_count, neighbors=neighbors, w_self=w_self, w_neigh=w_neigh, bias_hidden=bias_hidden, w_out=w_out, bias_out=bias_out, tiles=tiles, tile_rows=tile_rows, tile_cols=tile_cols, tile_count=tile_count, dangling=dangling)


teleport = 0.1
highest = lax.Precision.HIGHEST


def spread_rows(carried, tiles, tile_rows, tile_cols, tile_count):
    blocked = carried.reshape(PARTITIONS, GRID_COLS, NODE_DEV, C)
    slot_ids = jnp.arange(TMAX)
    levels = jnp.arange(ROW_TILES)

    def for_device(index_row, index_col):
        column_panel = jnp.take(blocked, index_col, axis=1).reshape(COL_TILES, TILE, C)
        blocks = column_panel[tile_cols[index_row, index_col]]
        usable = (slot_ids < tile_count[index_row, index_col]).astype(jnp.float32)
        matrices = tiles[index_row, index_col].astype(jnp.float32) * usable[:, None, None]
        product = jnp.einsum("tuv,tvc->tuc", matrices, blocks, precision=highest)
        placing = (tile_rows[index_row, index_col][:, None] == levels[None, :]).astype(jnp.float32)
        placed = jnp.einsum("tr,tuc->ruc", placing, product, precision=highest)
        return placed.reshape(ROW_TILES * TILE, C)

    def for_partition(index_row):
        pieces = jax.vmap(lambda index_col: for_device(index_row, index_col))(jnp.arange(GRID_COLS))
        return jnp.sum(pieces, axis=0)

    rows_out = lax.map(for_partition, jnp.arange(PARTITIONS))
    return rows_out.reshape(NODES, C)


def reference(features, send_rows, send_count, neighbors, w_self, w_neigh, bias_hidden, w_out, bias_out, tiles, tile_rows, tile_cols, tile_count, dangling):
    grouped = features.reshape(PARTITIONS, GRID_COLS, NODE_DEV, F)
    outgoing = jax.vmap(jax.vmap(lambda rows_here, picked: rows_here[picked]))(grouped, send_rows)
    slot_used = jnp.arange(CAP)[None, None, None, :] < send_count[:, :, :, None]
    outgoing = jnp.where(slot_used[..., None], outgoing, jnp.zeros((), jnp.bfloat16))
    received = jnp.transpose(outgoing, (2, 1, 0, 3, 4)).reshape(PARTITIONS, GRID_COLS, PARTITIONS * CAP, F)
    row_pool = jnp.concatenate([grouped, received], axis=2)
    linked = neighbors.reshape(PARTITIONS, GRID_COLS, NODE_DEV, DEG)
    fetched = jax.vmap(jax.vmap(lambda pool_here, picked: pool_here[picked]))(row_pool, linked)
    aggregate = (jnp.sum(fetched.astype(jnp.float32), axis=3) / DEG).astype(jnp.bfloat16).reshape(NODES, F)
    hidden = jax.nn.relu(jnp.dot(features, w_self, preferred_element_type=jnp.float32) + jnp.dot(aggregate, w_neigh, preferred_element_type=jnp.float32) + bias_hidden)
    logits = jnp.dot(hidden, w_out.astype(jnp.float32), precision=highest) + bias_out
    weight_mask = dangling.astype(jnp.float32)
    carried = logits
    for repeat in range(ITERS):
        dangling_sum = jnp.dot(weight_mask, carried, precision=highest)
        spread = spread_rows(carried, tiles, tile_rows, tile_cols, tile_count)
        carried = (1.0 - teleport) * (spread + dangling_sum[None, :] / NODES) + teleport * logits
    return carried
```

```python
import functools

import jax
import jax.numpy as jnp
from jax import lax
from jax.experimental import pallas as pl
from jax.experimental.pallas import tpu as pltpu
from jax.sharding import Mesh
from jax.sharding import PartitionSpec as P

ITERS = 3
TELEPORT = 0.1
TOP = 32767.0
TINY = 1e-30
INTERPRET = False

f32 = jnp.float32
bf16 = jnp.bfloat16
i32 = jnp.int32
i16 = jnp.int16


def call(body, out_shape, n_in, scratch=(), in_specs=None, flops=0, nbytes=0, limit=24 << 20):
    vmem = pl.BlockSpec(memory_space=pltpu.VMEM)
    outs = out_shape if isinstance(out_shape, (list, tuple)) else [out_shape]
    return pl.pallas_call(
        body,
        out_shape=out_shape,
        in_specs=in_specs or [vmem] * n_in,
        out_specs=[vmem] * len(outs) if isinstance(out_shape, (list, tuple)) else vmem,
        scratch_shapes=list(scratch),
        compiler_params=pltpu.CompilerParams(vmem_limit_bytes=limit),
        cost_estimate=pl.CostEstimate(flops=flops, bytes_accessed=nbytes, transcendentals=0),
        interpret=INTERPRET,
    )


def dot(a, b, dims=((1,), (0,))):
    return lax.dot_general(a, b, (dims, ((), ())), preferred_element_type=f32)


def split(x):
    hi = x.astype(bf16)
    return hi, (x - hi.astype(f32)).astype(bf16)


def encode(z, s, dangling, out_ref):
    nodes = z.shape[0]
    top = jnp.max(jnp.abs(z), axis=0, keepdims=True)
    dsum = jnp.sum(z * dangling[:nodes], axis=0, keepdims=True)
    ssum = jnp.sum(s * dangling[nodes : nodes + 1], axis=1, keepdims=True)
    row = lax.broadcasted_iota(i32, (8, z.shape[1]), 0)
    extra = jnp.where(row == 0, top, 0.0)
    extra = jnp.where(row == 1, s, extra)
    extra = jnp.where(row == 2, dsum, extra)
    extra = jnp.where(row == 3, ssum, extra)
    level = jnp.ceil(jnp.log2(jnp.maximum(jnp.abs(extra), TINY)) * 256.0)
    level = jnp.minimum(level, TOP)
    gain = TOP * jnp.exp2(level * (-1.0 / 256.0))
    codes = jnp.clip(jnp.round(z * gain[0:1]), -TOP, TOP).astype(i32)
    extra_codes = jnp.clip(jnp.round(extra * gain), -TOP, TOP).astype(i32)
    packed = jnp.concatenate([codes, level.astype(i32), extra_codes], axis=0).astype(i16)
    for k in range(out_ref.shape[0]):
        out_ref[k] = packed


def pick_kernel(index_ref, features_ref, out_ref):
    features = features_ref[...]
    nodes = features.shape[0]
    for k in range(index_ref.shape[0]):
        row = lax.broadcasted_iota(i32, (nodes, 128), 0)
        chosen = (row == index_ref[k : k + 1, :]).astype(f32).astype(bf16)
        out_ref[pl.ds(k * 128, 128), :] = dot(chosen, features, ((0,), (0,))).astype(bf16)


def panel_kernel(
    rows_ref, cols_ref, count_ref, tiles_ref, neighbors_ref, panel_ref, own_ref, far_ref, total
):
    row_tiles = panel_ref.shape[0] // 256
    col_tiles = panel_ref.shape[1] // 128
    zero = jnp.zeros((128, 128), f32)

    def clear(p, _):
        total[p] = zero
        return 0

    lax.fori_loop(0, row_tiles * col_tiles, clear, 0)

    def place(t, _):
        p = rows_ref[t] * col_tiles + cols_ref[t]
        total[p] = total[p] + tiles_ref[t].astype(f32)
        return 0

    lax.fori_loop(0, count_ref[0], place, 0)

    def store(r, _):
        for c in range(col_tiles):
            hi, lo = split(total[r * col_tiles + c])
            panel_ref[pl.ds(pl.multiple_of(r * 128, 128), 128), pl.ds(c * 128, 128)] = hi
            panel_ref[
                pl.ds(pl.multiple_of((r + row_tiles) * 128, 128), 128), pl.ds(c * 128, 128)
            ] = lo
        return 0

    lax.fori_loop(0, row_tiles, store, 0)

    nodes = own_ref.shape[0]
    degree = neighbors_ref.shape[1]
    linked = neighbors_ref[...]

    def counts(width, offset):
        slot = lax.broadcasted_iota(i32, (nodes, width), 1) + offset
        got = jnp.zeros((nodes, width), f32)
        for k in range(degree):
            got = got + jnp.where(linked[:, k : k + 1] == slot, 1.0, 0.0)
        return got.astype(bf16)

    own_ref[...] = counts(nodes, 0)
    for c in range(0, far_ref.shape[1], 256):
        far_ref[:, pl.ds(c, 256)] = counts(256, nodes + c)


def hidden_kernel(
    degree,
    features_ref,
    received_ref,
    own_ref,
    far_ref,
    w_self_ref,
    w_neigh_ref,
    bias_ref,
    dangling_ref,
    hidden_ref,
    out_ref,
):
    features = features_ref[...]
    pooled = dot(own_ref[...], features) + dot(far_ref[...], received_ref[...])
    aggregate = (pooled * (1.0 / degree)).astype(bf16)
    hidden = dot(features, w_self_ref[...]) + dot(aggregate, w_neigh_ref[...]) + bias_ref[...]
    hidden = jnp.maximum(hidden, 0.0)
    hidden_ref[...] = hidden
    encode(hidden, jnp.ones((1, hidden.shape[1]), f32), dangling_ref[...], out_ref)


def spread_kernel(
    node_total, parts, panel_hbm, packed_ref, out_ref, panel, z_parts, s_parts, sems
):
    zh, zl, nx = parts
    half = panel.shape[0] // 2
    loads = [
        pltpu.make_async_copy(
            panel_hbm.at[pl.ds(k * half, half)], panel.at[pl.ds(k * half, half)], sems.at[k]
        )
        for k in range(2)
    ]
    for load in loads:
        load.start()
    nodes = 64
    d_all = jnp.zeros((1, 128), f32)
    ds_all = jnp.zeros((1, 128), f32)
    lane = lax.broadcasted_iota(i32, (1, 128), 1)
    before = None
    for a in range(zh * zl * nx):
        h, m, x = a // (zl * nx), (a // nx) % zl, a % nx
        codes = packed_ref[x, m, h].astype(i32).astype(f32)
        step = jnp.exp2(codes[nodes : nodes + 8] * (1.0 / 256.0)) * (1.0 / TOP)
        hi, lo = split(codes[:nodes] * step[0:1])
        z_parts[pl.ds(a * nodes, nodes), pl.ds(0, 128)] = hi
        z_parts[pl.ds(a * nodes, nodes), pl.ds(128, 128)] = lo
        extra = codes[nodes + 8 : nodes + 16] * step
        d_all = d_all + extra[2:3]
        ds_all = ds_all + extra[3:4]
        if a % 2:
            hi, lo = split(jnp.where(lane < nodes, before, extra[1:2]))
            s_parts[:, pl.ds((a // 2) * 128, 128)] = jnp.concatenate(
                [hi.astype(f32), lo.astype(f32), jnp.zeros((14, 128), f32)], axis=0
            ).astype(bf16)
        before = extra[1:2]
    d_all = d_all * (1.0 / node_total)
    ds_all = ds_all * (1.0 / node_total)
    loads[0].wait()
    first = dot(panel[:half], z_parts[...])
    loads[1].wait()
    second = dot(panel[half:], z_parts[...])
    z_sum = (first[:, :128] + first[:, 128:]) + (second[:, :128] + second[:, 128:]) + d_all
    s_sum = dot(s_parts[...], panel[...], ((1,), (1,)))
    s_sum = (s_sum[0:1] + s_sum[1:2])
    s_sum = s_sum[:, :half] + s_sum[:, half:]
    for b in range(half // nodes):
        out_ref[b, pl.ds(0, nodes), :] = z_sum[b * nodes : (b + 1) * nodes]
        two = s_sum[:, (b // 2) * 128 : (b // 2) * 128 + 128]
        if b % 2:
            two = pltpu.roll(two, nodes, 1)
        out_ref[b, pl.ds(nodes, 8), :] = jnp.broadcast_to(two + ds_all, (8, 128))


def gather_step(received_ref, hidden_ref):
    nodes = hidden_ref.shape[0]
    total = received_ref[0]
    for j in range(1, received_ref.shape[0]):
        total = total + received_ref[j]
    z = (1.0 - TELEPORT) * total[:nodes] + TELEPORT * hidden_ref[...]
    s = (1.0 - TELEPORT) * total[nodes : nodes + 1] + TELEPORT
    return z, s


def step_kernel(received_ref, hidden_ref, dangling_ref, out_ref):
    z, s = gather_step(received_ref, hidden_ref)
    s8 = jnp.broadcast_to(s, (8, 128))
    lane = lax.broadcasted_iota(i32, (8, 128), 1)
    s8 = jnp.where(lane < z.shape[0], s8, pltpu.roll(s8, z.shape[0], 1))
    encode(z, s8[0:1], dangling_ref[...], out_ref)


def last_kernel(received_ref, hidden_ref, w_ref, bias_ref, out_ref):
    z, s = gather_step(received_ref, hidden_ref)
    nodes = z.shape[0]
    hi = z.astype(bf16)
    mid, lo = split(z - hi.astype(f32))
    w = w_ref[...]
    same = lax.broadcasted_iota(i32, (nodes, 128), 0) == lax.broadcasted_iota(i32, (nodes, 128), 1)
    column = jnp.sum(jnp.where(same, jnp.broadcast_to(s, (nodes, 128)), 0.0), axis=1, keepdims=True)
    out_ref[...] = (dot(lo, w) + dot(mid, w)) + dot(hi, w) + column * bias_ref[...]


def body(
    features,
    send_rows,
    send_count,
    neighbors,
    w_self,
    w_neigh,
    bias_hidden,
    w_out,
    bias_out,
    tiles,
    tile_rows,
    tile_cols,
    tile_count,
    dangling,
):
    shape = jax.ShapeDtypeStruct
    nodes, width = features.shape
    zh, zl, nx = (lax.axis_size(name) for name in ("zh", "zl", "x"))
    wide = zh * zl * nx
    narrow = lax.axis_size("narrow")
    capacity = send_rows.shape[-1]
    slots = wide * capacity
    row_total = narrow * nodes
    col_total = wide * nodes
    node_total = row_total * wide
    degree = neighbors.shape[1]

    used = jnp.arange(capacity)[None, :] < send_count[0, 0][:, None]
    index = jnp.where(used, send_rows[0, 0], -1).reshape(slots // 128, 128)
    outgoing = call(pick_kernel, shape((slots, width), bf16), 2)(index, features)
    received = lax.all_to_all(
        outgoing.reshape(wide, capacity, width),
        ("zh", "zl", "x"),
        split_axis=0,
        concat_axis=0,
        tiled=True,
    ).reshape(slots, width)

    smem = pl.BlockSpec(memory_space=pltpu.SMEM)
    vmem = pl.BlockSpec(memory_space=pltpu.VMEM)
    panel, own, far = call(
        panel_kernel,
        [
            shape((2 * row_total, col_total), bf16),
            shape((nodes, nodes), bf16),
            shape((nodes, slots), bf16),
        ],
        5,
        in_specs=[smem, smem, smem, vmem, vmem],
        scratch=[pltpu.VMEM((row_total * col_total // (128 * 128), 128, 128), f32)],
        flops=1 << 24,
        nbytes=20 << 20,
        limit=28 << 20,
    )(tile_rows[0, 0], tile_cols[0, 0], tile_count[0], tiles[0, 0], neighbors)

    mark = dangling.astype(f32)
    marks = jnp.concatenate(
        [
            jnp.broadcast_to(mark[:, None], (nodes, 128)),
            jnp.broadcast_to(jnp.pad(mark, (0, 128 - nodes))[None, :], (8, 128)),
        ],
        axis=0,
    )

    packed_shape = shape((zh, nodes + 16, width), i16)
    hidden, packed = call(
        functools.partial(hidden_kernel, degree),
        [shape((nodes, width), f32), packed_shape],
        8,
    )(features, received, own, far, w_self, w_neigh, bias_hidden[None, :], marks)

    spread = call(
        functools.partial(spread_kernel, node_total, (zh, zl, nx)),
        shape((narrow, nodes + 8, width), f32),
        2,
        in_specs=[pl.BlockSpec(memory_space=pl.ANY), vmem],
        scratch=[
            pltpu.VMEM((2 * row_total, col_total), bf16),
            pltpu.VMEM((col_total, 2 * width), bf16),
            pltpu.VMEM((16, col_total), bf16),
            pltpu.SemaphoreType.DMA((2,)),
        ],
        flops=2 * 2 * row_total * col_total * 256,
        nbytes=10 << 20,
    )
    for repeat in range(ITERS):
        got = lax.all_to_all(packed, "zh", split_axis=0, concat_axis=0, tiled=True)
        got = lax.all_to_all(
            jnp.broadcast_to(got[None], (zl,) + got.shape),
            "zl",
            split_axis=0,
            concat_axis=0,
            tiled=True,
        )
        got = lax.all_gather(got, "x", axis=0)
        partial = spread(panel, got)
        sums = lax.all_to_all(partial, "narrow", split_axis=0, concat_axis=0, tiled=True)
        if repeat < ITERS - 1:
            packed = call(step_kernel, packed_shape, 3)(sums, hidden, marks)
    return call(last_kernel, shape((nodes, w_out.shape[1]), f32), 4)(
        sums, hidden, w_out, bias_out[None, :]
    )


def solution(mesh):
    wide, narrow = mesh.devices.shape
    nx = 4 if wide % 64 == 0 else 2
    zl = 4 if wide % 64 == 0 else 2
    split_mesh = Mesh(
        mesh.devices.reshape(wide // (zl * nx), zl, nx, narrow), ("zh", "zl", "x", "narrow")
    )
    wide_axes = ("zh", "zl", "x")
    all_axes = wide_axes + ("narrow",)
    in_specs = (
        P(all_axes, None),
        P(wide_axes, "narrow", None, None),
        P(wide_axes, "narrow", None),
        P(all_axes, None),
        P(),
        P(),
        P(),
        P(),
        P(),
        P(wide_axes, "narrow", None, None, None),
        P(wide_axes, "narrow", None),
        P(wide_axes, "narrow", None),
        P(wide_axes, "narrow"),
        P(all_axes),
    )
    return jax.shard_map(
        body, mesh=split_mesh, in_specs=in_specs, out_specs=P(all_axes, None), check_vma=False
    )
```

```python
import functools

import jax
import jax.numpy as jnp
from jax import lax
from jax.experimental import pallas as pl
from jax.experimental.pallas import tpu as pltpu
from jax.sharding import Mesh
from jax.sharding import PartitionSpec as P

ITERS = 3
TELEPORT = 0.1
TOP = 32767.0
TINY = 1e-30
INTERPRET = False

f32 = jnp.float32
bf16 = jnp.bfloat16
i32 = jnp.int32
i16 = jnp.int16


def call(body, out_shape, n_in, scratch=(), in_specs=None, flops=0, nbytes=0, limit=24 << 20):
    vmem = pl.BlockSpec(memory_space=pltpu.VMEM)
    outs = out_shape if isinstance(out_shape, (list, tuple)) else [out_shape]
    return pl.pallas_call(
        body,
        out_shape=out_shape,
        in_specs=in_specs or [vmem] * n_in,
        out_specs=[vmem] * len(outs) if isinstance(out_shape, (list, tuple)) else vmem,
        scratch_shapes=list(scratch),
        compiler_params=pltpu.CompilerParams(vmem_limit_bytes=limit),
        cost_estimate=pl.CostEstimate(flops=flops, bytes_accessed=nbytes, transcendentals=0),
        interpret=INTERPRET,
    )


def dot(a, b, dims=((1,), (0,))):
    return lax.dot_general(a, b, (dims, ((), ())), preferred_element_type=f32)


def split(x):
    hi = x.astype(bf16)
    return hi, (x - hi.astype(f32)).astype(bf16)


def lane_sums(x):
    ones = jnp.ones((8, x.shape[1]), bf16)
    hi, rest = x.astype(bf16), x - x.astype(bf16).astype(f32)
    mid, lo = split(rest)
    over = ((1,), (1,))
    return (dot(ones, lo, over) + dot(ones, mid, over)) + dot(ones, hi, over)


def encode(z, s, dangling, out_ref):
    nodes = z.shape[0]
    top = jnp.max(jnp.abs(z), axis=0, keepdims=True)
    dsum = jnp.sum(z * dangling[:nodes], axis=0, keepdims=True)
    ssum = jnp.sum(s * dangling[nodes : nodes + 1], axis=1, keepdims=True)
    row = lax.broadcasted_iota(i32, (8, z.shape[1]), 0)
    extra = jnp.where((row & 3) == 0, top, 0.0)
    extra = jnp.where((row & 3) == 1, s, extra)
    extra = jnp.where((row & 3) == 2, dsum, extra)
    extra = jnp.where((row & 3) == 3, ssum, extra)
    level = jnp.ceil(jnp.log2(jnp.maximum(jnp.abs(extra), TINY)) * 256.0)
    level = jnp.minimum(level, TOP)
    gain = TOP * jnp.exp2(level * (-1.0 / 256.0))
    codes = jnp.clip(jnp.round(z * gain[0:1]), -TOP, TOP)
    extra_codes = jnp.clip(jnp.round(extra * gain), -TOP, TOP)
    tail = jnp.where(row < 4, level, extra_codes)
    packed = jnp.concatenate([codes, tail], axis=0).astype(i32).astype(i16)
    for k in range(out_ref.shape[0]):
        out_ref[k] = packed


def pick_kernel(count_ref, index_ref, features_ref, out_ref):
    features = features_ref[...]
    nodes = features.shape[0]
    capacity = out_ref.shape[0] // count_ref.shape[0]
    per_row = 128 // capacity
    lane = lax.broadcasted_iota(i32, (1, 128), 1)
    row = lax.broadcasted_iota(i32, (nodes, 128), 0)
    for k in range(index_ref.shape[0]):
        end = count_ref[k * per_row]
        for m in range(1, per_row):
            end = jnp.where(lane >= m * capacity, count_ref[k * per_row + m] + m * capacity, end)
        index = jnp.where(lane < end, index_ref[k : k + 1, :], -1)
        chosen = (row == index).astype(f32).astype(bf16)
        out_ref[pl.ds(k * 128, 128), :] = dot(chosen, features, ((0,), (0,))).astype(bf16)


def panel_kernel(
    rows_ref,
    cols_ref,
    count_ref,
    tiles_ref,
    neighbors_ref,
    panel_ref,
    sums_ref,
    own_ref,
    far_ref,
    total,
):
    row_tiles = panel_ref.shape[0] // 256
    col_tiles = panel_ref.shape[1] // 128
    zero = jnp.zeros((128, 128), f32)

    def clear(p, _):
        total[p] = zero
        return 0

    lax.fori_loop(0, row_tiles * col_tiles, clear, 0)

    def place(t, _):
        p = rows_ref[t] * col_tiles + cols_ref[t]
        total[p] = total[p] + tiles_ref[t].astype(f32)
        return 0

    lax.fori_loop(0, count_ref[0], place, 0)

    for r in range(row_tiles):
        whole = total[r * col_tiles]
        for c in range(1, col_tiles):
            whole = whole + total[r * col_tiles + c]
        sums_ref[:, pl.ds(r * 128, 128)] = lane_sums(whole)

    def store(r, _):
        for c in range(col_tiles):
            hi, lo = split(total[r * col_tiles + c])
            panel_ref[pl.ds(pl.multiple_of(r * 128, 128), 128), pl.ds(c * 128, 128)] = hi
            panel_ref[
                pl.ds(pl.multiple_of((r + row_tiles) * 128, 128), 128), pl.ds(c * 128, 128)
            ] = lo
        return 0

    lax.fori_loop(0, row_tiles, store, 0)

    nodes = own_ref.shape[0]
    degree = neighbors_ref.shape[1]
    linked = neighbors_ref[...]

    def counts(width, offset):
        slot = lax.broadcasted_iota(i32, (nodes, width), 1) + offset
        got = jnp.zeros((nodes, width), f32)
        for k in range(degree):
            got = got + jnp.where(linked[:, k : k + 1] == slot, 1.0, 0.0)
        return got.astype(bf16)

    own_ref[...] = counts(nodes, 0)
    for c in range(0, far_ref.shape[1], 256):
        far_ref[:, pl.ds(c, 256)] = counts(256, nodes + c)


def hidden_kernel(
    degree,
    features_ref,
    received_ref,
    own_ref,
    far_ref,
    w_self_ref,
    w_neigh_ref,
    bias_ref,
    dangling_ref,
    hidden_ref,
    out_ref,
):
    features = features_ref[...]
    pooled = dot(own_ref[...], features) + dot(far_ref[...], received_ref[...])
    aggregate = (pooled * (1.0 / degree)).astype(bf16)
    hidden = dot(features, w_self_ref[...]) + dot(aggregate, w_neigh_ref[...]) + bias_ref[...]
    hidden = jnp.maximum(hidden, 0.0)
    hidden_ref[...] = hidden
    encode(hidden, jnp.ones((1, hidden.shape[1]), f32), dangling_ref[...], out_ref)


def spread_kernel(node_total, parts, first, panel_ref, sums_ref, packed_ref, out_ref, z_parts, s_row):
    zh, zl, nx = parts
    half = panel_ref.shape[0] // 2
    nodes = 64
    d_all = jnp.zeros((1, 128), f32)
    ds_all = jnp.zeros((1, 128), f32)
    lane = lax.broadcasted_iota(i32, (1, 128), 1)
    before = None
    for a in range(zh * zl * nx):
        h, m, x = a // (zl * nx), (a // nx) % zl, a % nx
        codes = packed_ref[x, m, h].astype(i32).astype(f32)
        tail = codes[nodes:]
        step = jnp.exp2(tail * (1.0 / 256.0)) * (1.0 / TOP)
        hi, lo = split(codes[:nodes] * step[0:1])
        z_parts[pl.ds(a * nodes, nodes), pl.ds(0, 128)] = hi
        z_parts[pl.ds(a * nodes, nodes), pl.ds(128, 128)] = lo
        extra = pltpu.roll(tail, 4, 0) * step
        d_all = d_all + extra[2:3]
        ds_all = ds_all + extra[3:4]
        if a % 2 and not first:
            s_row[0:1, pl.ds((a // 2) * 128, 128)] = jnp.where(lane < nodes, before, extra[1:2])
        before = extra[1:2]
    d_all = d_all * (1.0 / node_total)
    ds_all = ds_all * (1.0 / node_total)
    upper = dot(panel_ref[:half], z_parts[...])
    lower = dot(panel_ref[half:], z_parts[...])
    z_sum = (upper[:, :128] + upper[:, 128:]) + (lower[:, :128] + lower[:, 128:]) + d_all
    if first:
        s_sum = sums_ref[...]
    else:
        part = jnp.zeros((half, 128), f32)
        for c in range(panel_ref.shape[1] // 128):
            at = pl.ds(c * 128, 128)
            tile = panel_ref[:half, at].astype(f32) + panel_ref[half:, at].astype(f32)
            part = part + tile * s_row[0:1, at]
        s_sum = lane_sums(part)
    for b in range(half // nodes):
        out_ref[b, pl.ds(0, nodes), :] = z_sum[b * nodes : (b + 1) * nodes]
        two = s_sum[:, (b // 2) * 128 : (b // 2) * 128 + 128]
        if b % 2:
            two = pltpu.roll(two, nodes, 1)
        out_ref[b, pl.ds(nodes, 8), :] = two + ds_all


def gather_step(received_ref, hidden_ref):
    nodes = hidden_ref.shape[0]
    total = received_ref[0]
    for j in range(1, received_ref.shape[0]):
        total = total + received_ref[j]
    z = (1.0 - TELEPORT) * total[:nodes] + TELEPORT * hidden_ref[...]
    s = (1.0 - TELEPORT) * total[nodes : nodes + 1] + TELEPORT
    return z, s


def step_kernel(received_ref, hidden_ref, dangling_ref, out_ref):
    z, s = gather_step(received_ref, hidden_ref)
    s8 = jnp.broadcast_to(s, (8, 128))
    lane = lax.broadcasted_iota(i32, (8, 128), 1)
    s8 = jnp.where(lane < z.shape[0], s8, pltpu.roll(s8, z.shape[0], 1))
    encode(z, s8[0:1], dangling_ref[...], out_ref)


def last_kernel(received_ref, hidden_ref, w_ref, bias_ref, out_ref):
    z, s = gather_step(received_ref, hidden_ref)
    nodes = z.shape[0]
    hi = z.astype(bf16)
    mid, lo = split(z - hi.astype(f32))
    w = w_ref[...]
    same = lax.broadcasted_iota(i32, (nodes, 128), 0) == lax.broadcasted_iota(i32, (nodes, 128), 1)
    column = jnp.sum(jnp.where(same, jnp.broadcast_to(s, (nodes, 128)), 0.0), axis=1, keepdims=True)
    out_ref[...] = (dot(lo, w) + dot(mid, w)) + dot(hi, w) + column * bias_ref[...]


def body(
    features,
    send_rows,
    send_count,
    neighbors,
    w_self,
    w_neigh,
    bias_hidden,
    w_out,
    bias_out,
    tiles,
    tile_rows,
    tile_cols,
    tile_count,
    dangling,
):
    shape = jax.ShapeDtypeStruct
    nodes, width = features.shape
    zh, zl, nx = (lax.axis_size(name) for name in ("zh", "zl", "x"))
    wide = zh * zl * nx
    narrow = lax.axis_size("narrow")
    capacity = send_rows.shape[-1]
    slots = wide * capacity
    row_total = narrow * nodes
    col_total = wide * nodes
    node_total = row_total * wide
    degree = neighbors.shape[1]

    smem = pl.BlockSpec(memory_space=pltpu.SMEM)
    vmem = pl.BlockSpec(memory_space=pltpu.VMEM)
    outgoing = call(
        pick_kernel, shape((slots, width), bf16), 3, in_specs=[smem, vmem, vmem], limit=8 << 20
    )(send_count[0, 0], send_rows[0, 0].reshape(slots // 128, 128), features)
    panel, row_sums, own, far = call(
        panel_kernel,
        [
            shape((2 * row_total, col_total), bf16),
            shape((8, row_total), f32),
            shape((nodes, nodes), bf16),
            shape((nodes, slots), bf16),
        ],
        5,
        in_specs=[smem, smem, smem, vmem, vmem],
        scratch=[pltpu.VMEM((row_total * col_total // (128 * 128), 128, 128), f32)],
        flops=1 << 24,
        nbytes=20 << 20,
        limit=14 << 20,
    )(tile_rows[0, 0], tile_cols[0, 0], tile_count[0], tiles[0, 0], neighbors)

    mark = dangling.astype(f32)
    marks = jnp.concatenate(
        [
            jnp.broadcast_to(mark[:, None], (nodes, 128)),
            jnp.broadcast_to(jnp.pad(mark, (0, 128 - nodes))[None, :], (8, 128)),
        ],
        axis=0,
    )

    outgoing, panel, row_sums, own, far, marks = lax.optimization_barrier(
        (outgoing, panel, row_sums, own, far, marks)
    )
    received = lax.all_to_all(
        outgoing.reshape(wide, capacity, width),
        ("zh", "zl", "x"),
        split_axis=0,
        concat_axis=0,
        tiled=True,
    ).reshape(slots, width)

    packed_shape = shape((zh, nodes + 8, width), i16)
    hidden, packed = call(
        functools.partial(hidden_kernel, degree),
        [shape((nodes, width), f32), packed_shape],
        8,
        limit=8 << 20,
    )(features, received, own, far, w_self, w_neigh, bias_hidden[None, :], marks)

    def spread(packed, repeat):
        return call(
            functools.partial(spread_kernel, node_total, (zh, zl, nx), repeat == 0),
            shape((narrow, nodes + 8, width), f32),
            3,
            scratch=[pltpu.VMEM((col_total, 2 * width), bf16), pltpu.VMEM((8, col_total), f32)],
            flops=2 * 2 * row_total * col_total * 256,
            nbytes=10 << 20,
            limit=12 << 20,
        )(panel, row_sums, packed)

    for repeat in range(ITERS):
        got = lax.all_to_all(packed, "zh", split_axis=0, concat_axis=0, tiled=True)
        got = lax.all_to_all(
            jnp.broadcast_to(got[None], (zl,) + got.shape),
            "zl",
            split_axis=0,
            concat_axis=0,
            tiled=True,
        )
        got = lax.all_gather(got, "x", axis=0)
        partial = spread(got, repeat)
        sums = lax.all_to_all(partial, "narrow", split_axis=0, concat_axis=0, tiled=True)
        if repeat < ITERS - 1:
            packed = call(step_kernel, packed_shape, 3, limit=4 << 20)(sums, hidden, marks)
    return call(last_kernel, shape((nodes, w_out.shape[1]), f32), 4, limit=4 << 20)(
        sums, hidden, w_out, bias_out[None, :]
    )


def solution(mesh):
    wide, narrow = mesh.devices.shape
    nx = 4 if wide % 64 == 0 else 2
    zl = 4 if wide % 64 == 0 else 2
    split_mesh = Mesh(
        mesh.devices.reshape(wide // (zl * nx), zl, nx, narrow), ("zh", "zl", "x", "narrow")
    )
    wide_axes = ("zh", "zl", "x")
    all_axes = wide_axes + ("narrow",)
    in_specs = (
        P(all_axes, None),
        P(wide_axes, "narrow", None, None),
        P(wide_axes, "narrow", None),
        P(all_axes, None),
        P(),
        P(),
        P(),
        P(),
        P(),
        P(wide_axes, "narrow", None, None, None),
        P(wide_axes, "narrow", None),
        P(wide_axes, "narrow", None),
        P(wide_axes, "narrow"),
        P(all_axes),
    )
    return jax.shard_map(
        body, mesh=split_mesh, in_specs=in_specs, out_specs=P(all_axes, None), check_vma=False
    )
```

```python
import functools

import jax
import jax.numpy as jnp
from jax import lax
from jax.experimental import pallas as pl
from jax.experimental.pallas import tpu as pltpu
from jax.sharding import Mesh
from jax.sharding import PartitionSpec as P

ITERS = 3
TELEPORT = 0.1
TOP = 32767.0
TINY = 1e-30
INTERPRET = False

f32 = jnp.float32
bf16 = jnp.bfloat16
i32 = jnp.int32
i16 = jnp.int16


def call(body, out_shape, n_in, scratch=(), in_specs=None, flops=0, nbytes=0, limit=24 << 20):
    vmem = pl.BlockSpec(memory_space=pltpu.VMEM)
    outs = out_shape if isinstance(out_shape, (list, tuple)) else [out_shape]
    return pl.pallas_call(
        body,
        out_shape=out_shape,
        in_specs=in_specs or [vmem] * n_in,
        out_specs=[vmem] * len(outs) if isinstance(out_shape, (list, tuple)) else vmem,
        scratch_shapes=list(scratch),
        compiler_params=pltpu.CompilerParams(vmem_limit_bytes=limit),
        cost_estimate=pl.CostEstimate(flops=flops, bytes_accessed=nbytes, transcendentals=0),
        interpret=INTERPRET,
    )


def dot(a, b, dims=((1,), (0,))):
    return lax.dot_general(a, b, (dims, ((), ())), preferred_element_type=f32)


def split(x):
    hi = x.astype(bf16)
    return hi, (x - hi.astype(f32)).astype(bf16)


def lane_sums(x):
    ones = jnp.ones((8, x.shape[1]), bf16)
    hi, rest = x.astype(bf16), x - x.astype(bf16).astype(f32)
    mid, lo = split(rest)
    over = ((1,), (1,))
    return (dot(ones, lo, over) + dot(ones, mid, over)) + dot(ones, hi, over)


def encode(z, s, dangling, out_ref):
    nodes = z.shape[0]
    top = jnp.max(jnp.abs(z), axis=0, keepdims=True)
    dsum = jnp.sum(z * dangling[:nodes], axis=0, keepdims=True)
    ssum = jnp.sum(s * dangling[nodes : nodes + 1], axis=1, keepdims=True)
    row = lax.broadcasted_iota(i32, (8, z.shape[1]), 0)
    extra = jnp.where((row & 3) == 0, top, 0.0)
    extra = jnp.where((row & 3) == 1, s, extra)
    extra = jnp.where((row & 3) == 2, dsum, extra)
    extra = jnp.where((row & 3) == 3, ssum, extra)
    level = jnp.ceil(jnp.log2(jnp.maximum(jnp.abs(extra), TINY)) * 256.0)
    level = jnp.minimum(level, TOP)
    gain = TOP * jnp.exp2(level * (-1.0 / 256.0))
    codes = jnp.clip(jnp.round(z * gain[0:1]), -TOP, TOP)
    extra_codes = jnp.clip(jnp.round(extra * gain), -TOP, TOP)
    tail = jnp.where(row < 4, level, extra_codes)
    packed = jnp.concatenate([codes, tail], axis=0).astype(i32).astype(i16)
    for k in range(out_ref.shape[0]):
        out_ref[k] = packed


def head_kernel(
    count_hbm,
    send_hbm,
    features_hbm,
    rows_hbm,
    cols_hbm,
    used_hbm,
    tiles_hbm,
    linked_hbm,
    dangling_hbm,
    outgoing_ref,
    panel_ref,
    sums_ref,
    own_ref,
    far_ref,
    marks_ref,
    count_ref,
    send_ref,
    features_ref,
    rows_ref,
    cols_ref,
    used_ref,
    tiles_ref,
    linked_ref,
    dangling_ref,
    index_ref,
    total,
    sems,
):
    pairs = (
        (count_hbm, count_ref),
        (send_hbm, send_ref),
        (features_hbm, features_ref),
        (linked_hbm, linked_ref),
        (dangling_hbm, dangling_ref),
        (rows_hbm, rows_ref),
        (cols_hbm, cols_ref),
        (used_hbm, used_ref),
        (tiles_hbm, tiles_ref),
    )
    loads = [pltpu.make_async_copy(a, b, sems.at[k]) for k, (a, b) in enumerate(pairs)]
    for load in loads:
        load.start()

    row_tiles = panel_ref.shape[0] // 256
    col_tiles = panel_ref.shape[1] // 128
    zero = jnp.zeros((128, 128), f32)

    def clear(p, _):
        total[p] = zero
        return 0

    lax.fori_loop(0, row_tiles * col_tiles, clear, 0)
    for load in loads[:5]:
        load.wait()

    features = features_ref[...]
    nodes = features.shape[0]
    lists, capacity = send_ref.shape
    per_row = 128 // capacity
    lane = lax.broadcasted_iota(i32, (1, 128), 1)
    row = lax.broadcasted_iota(i32, (nodes, 128), 0)
    for m in range(per_row):
        index_ref[:, pl.ds(m * capacity, capacity)] = send_ref[
            pl.ds(m, lists // per_row, stride=per_row), :
        ]
    for k in range(lists // per_row):
        end = count_ref[0, k * per_row]
        for m in range(1, per_row):
            end = jnp.where(lane >= m * capacity, count_ref[0, k * per_row + m] + m * capacity, end)
        index = jnp.where(lane < end, index_ref[k : k + 1, :], -1)
        chosen = (row == index).astype(f32).astype(bf16)
        outgoing_ref[pl.ds(k * 128, 128), :] = dot(chosen, features, ((0,), (0,))).astype(bf16)

    same = lax.broadcasted_iota(i32, (nodes, nodes), 0) == lax.broadcasted_iota(
        i32, (nodes, nodes), 1
    )
    eye = same.astype(f32).astype(bf16)
    linked = linked_ref[...]
    high = linked >> 6
    over = ((1,), (1,))
    linked = 64.0 * dot(eye, high.astype(f32).astype(bf16), over) + dot(
        eye, (linked - (high << 6)).astype(f32).astype(bf16), over
    )
    linked = linked.astype(i32)

    def counts(width, offset):
        slot = lax.broadcasted_iota(i32, (nodes, width), 1) + offset
        got = jnp.zeros((nodes, width), f32)
        for k in range(linked.shape[1]):
            got = got + jnp.where(linked[:, k : k + 1] == slot, 1.0, 0.0)
        return got.astype(bf16)

    own_ref[...] = counts(nodes, 0)
    for c in range(0, far_ref.shape[1], 256):
        far_ref[:, pl.ds(c, 256)] = counts(256, nodes + c)

    mark = dangling_ref[...].astype(f32)
    column = jnp.sum(jnp.where(same, jnp.broadcast_to(mark, same.shape), 0.0), axis=1, keepdims=True)
    marks_ref[pl.ds(0, nodes), :] = jnp.broadcast_to(column, (nodes, 128))
    marks_ref[pl.ds(nodes, 8), :] = jnp.zeros((8, 128), f32)
    marks_ref[pl.ds(nodes, 8), pl.ds(0, nodes)] = jnp.broadcast_to(mark, (8, nodes))

    for load in loads[5:]:
        load.wait()

    def place(t, _):
        p = rows_ref[0, t] * col_tiles + cols_ref[0, t]
        total[p] = total[p] + tiles_ref[t].astype(f32)
        return 0

    lax.fori_loop(0, used_ref[0, 0], place, 0)

    def store(r, _):
        at = pl.ds(pl.multiple_of(r * 128, 128), 128)
        below = pl.ds(pl.multiple_of((r + row_tiles) * 128, 128), 128)
        whole = jnp.zeros((128, 128), f32)
        for c in range(col_tiles):
            tile = total[r * col_tiles + c]
            whole = whole + tile
            panel_ref[at, pl.ds(c * 128, 128)], panel_ref[below, pl.ds(c * 128, 128)] = split(tile)
        sums_ref[:, at] = lane_sums(whole)
        return 0

    lax.fori_loop(0, row_tiles, store, 0)


def hidden_kernel(
    degree,
    features_ref,
    received_ref,
    own_ref,
    far_ref,
    w_self_ref,
    w_neigh_ref,
    bias_ref,
    dangling_ref,
    hidden_ref,
    out_ref,
):
    features = features_ref[...]
    pooled = dot(own_ref[...], features) + dot(far_ref[...], received_ref[...])
    aggregate = (pooled * (1.0 / degree)).astype(bf16)
    hidden = dot(features, w_self_ref[...]) + dot(aggregate, w_neigh_ref[...]) + bias_ref[...]
    hidden = jnp.maximum(hidden, 0.0)
    hidden_ref[...] = hidden
    encode(hidden, jnp.ones((1, hidden.shape[1]), f32), dangling_ref[...], out_ref)


def spread_kernel(node_total, parts, first, panel_ref, sums_ref, packed_ref, out_ref, z_parts, s_row):
    zh, zl, nx = parts
    half = panel_ref.shape[0] // 2
    nodes = 64
    d_all = jnp.zeros((1, 128), f32)
    ds_all = jnp.zeros((1, 128), f32)
    lane = lax.broadcasted_iota(i32, (1, 128), 1)
    before = None
    for a in range(zh * zl * nx):
        h, m, x = a // (zl * nx), (a // nx) % zl, a % nx
        codes = packed_ref[m, x, h].astype(i32).astype(f32)
        tail = codes[nodes:]
        step = jnp.exp2(tail * (1.0 / 256.0)) * (1.0 / TOP)
        hi, lo = split(codes[:nodes] * step[0:1])
        z_parts[pl.ds(a * nodes, nodes), pl.ds(0, 128)] = hi
        z_parts[pl.ds(a * nodes, nodes), pl.ds(128, 128)] = lo
        extra = pltpu.roll(tail, 4, 0) * step
        d_all = d_all + extra[2:3]
        ds_all = ds_all + extra[3:4]
        if a % 2 and not first:
            s_row[0:1, pl.ds((a // 2) * 128, 128)] = jnp.where(lane < nodes, before, extra[1:2])
        before = extra[1:2]
    d_all = d_all * (1.0 / node_total)
    ds_all = ds_all * (1.0 / node_total)
    upper = dot(panel_ref[:half], z_parts[...])
    lower = dot(panel_ref[half:], z_parts[...])
    z_sum = (upper[:, :128] + upper[:, 128:]) + (lower[:, :128] + lower[:, 128:]) + d_all
    if first:
        s_sum = sums_ref[...]
    else:
        part = jnp.zeros((half, 128), f32)
        for c in range(panel_ref.shape[1] // 128):
            at = pl.ds(c * 128, 128)
            tile = panel_ref[:half, at].astype(f32) + panel_ref[half:, at].astype(f32)
            part = part + tile * s_row[0:1, at]
        s_sum = lane_sums(part)
    for b in range(half // nodes):
        out_ref[b, pl.ds(0, nodes), :] = z_sum[b * nodes : (b + 1) * nodes]
        two = s_sum[:, (b // 2) * 128 : (b // 2) * 128 + 128]
        if b % 2:
            two = pltpu.roll(two, nodes, 1)
        out_ref[b, pl.ds(nodes, 8), :] = two + ds_all


def gather_step(received_ref, hidden_ref):
    nodes = hidden_ref.shape[0]
    total = received_ref[0]
    for j in range(1, received_ref.shape[0]):
        total = total + received_ref[j]
    z = (1.0 - TELEPORT) * total[:nodes] + TELEPORT * hidden_ref[...]
    s = (1.0 - TELEPORT) * total[nodes : nodes + 1] + TELEPORT
    return z, s


def step_kernel(received_ref, hidden_ref, dangling_ref, out_ref):
    z, s = gather_step(received_ref, hidden_ref)
    s8 = jnp.broadcast_to(s, (8, 128))
    lane = lax.broadcasted_iota(i32, (8, 128), 1)
    s8 = jnp.where(lane < z.shape[0], s8, pltpu.roll(s8, z.shape[0], 1))
    encode(z, s8[0:1], dangling_ref[...], out_ref)


def last_kernel(received_ref, hidden_ref, w_ref, bias_ref, out_ref):
    z, s = gather_step(received_ref, hidden_ref)
    nodes = z.shape[0]
    hi = z.astype(bf16)
    mid, lo = split(z - hi.astype(f32))
    w = w_ref[...]
    same = lax.broadcasted_iota(i32, (nodes, 128), 0) == lax.broadcasted_iota(i32, (nodes, 128), 1)
    column = jnp.sum(jnp.where(same, jnp.broadcast_to(s, (nodes, 128)), 0.0), axis=1, keepdims=True)
    out_ref[...] = (dot(lo, w) + dot(mid, w)) + dot(hi, w) + column * bias_ref[...]


def body(
    features,
    send_rows,
    send_count,
    neighbors,
    w_self,
    w_neigh,
    bias_hidden,
    w_out,
    bias_out,
    tiles,
    tile_rows,
    tile_cols,
    tile_count,
    dangling,
):
    shape = jax.ShapeDtypeStruct
    nodes, width = features.shape
    zh, zl, nx = (lax.axis_size(name) for name in ("zh", "zl", "x"))
    wide = zh * zl * nx
    narrow = lax.axis_size("narrow")
    capacity = send_rows.shape[-1]
    slots = wide * capacity
    row_total = narrow * nodes
    col_total = wide * nodes
    node_total = row_total * wide
    degree = neighbors.shape[1]

    outgoing, panel, row_sums, own, far, marks = call(
        head_kernel,
        [
            shape((slots, width), bf16),
            shape((2 * row_total, col_total), bf16),
            shape((8, row_total), f32),
            shape((nodes, nodes), bf16),
            shape((nodes, slots), bf16),
            shape((nodes + 8, 128), f32),
        ],
        9,
        in_specs=[pl.BlockSpec(memory_space=pltpu.HBM)] * 9,
        scratch=[
            pltpu.SMEM((1, wide), i32),
            pltpu.VMEM((wide, capacity), i32),
            pltpu.VMEM((nodes, width), bf16),
            pltpu.SMEM(tile_rows.shape[1:], i32),
            pltpu.SMEM(tile_rows.shape[1:], i32),
            pltpu.SMEM((1, 1), i32),
            pltpu.VMEM(tiles.shape[2:], bf16),
            pltpu.VMEM((degree, nodes), i32),
            pltpu.VMEM((1, nodes), i32),
            pltpu.VMEM((wide * capacity // 128, 128), i32),
            pltpu.VMEM((row_total * col_total // (128 * 128), 128, 128), f32),
            pltpu.SemaphoreType.DMA((9,)),
        ],
        flops=1 << 24,
        nbytes=20 << 20,
        limit=16 << 20,
    )(
        send_count[0],
        send_rows[0, 0],
        features,
        tile_rows[0],
        tile_cols[0],
        tile_count,
        tiles[0, 0],
        neighbors.T,
        dangling[None, :],
    )
    received = lax.all_to_all(
        outgoing.reshape(wide, capacity, width),
        ("zh", "zl", "x"),
        split_axis=0,
        concat_axis=0,
        tiled=True,
    ).reshape(slots, width)

    packed_shape = shape((zh, nodes + 8, width), i16)
    hidden, packed = call(
        functools.partial(hidden_kernel, degree),
        [shape((nodes, width), f32), packed_shape],
        8,
        limit=8 << 20,
    )(features, received, own, far, w_self, w_neigh, bias_hidden[None, :], marks)

    def spread(packed, repeat):
        return call(
            functools.partial(spread_kernel, node_total, (zh, zl, nx), repeat == 0),
            shape((narrow, nodes + 8, width), f32),
            3,
            scratch=[pltpu.VMEM((col_total, 2 * width), bf16), pltpu.VMEM((8, col_total), f32)],
            flops=2 * 2 * row_total * col_total * 256,
            nbytes=10 << 20,
            limit=12 << 20,
        )(panel, row_sums, packed)

    for repeat in range(ITERS):
        got = lax.all_to_all(packed, "zh", split_axis=0, concat_axis=0, tiled=True)
        if repeat == 1:
            got = lax.all_gather(got, ("zl", "x"), axis=0)
        else:
            got = lax.all_to_all(
                jnp.broadcast_to(got[None], (zl * nx,) + got.shape),
                ("zl", "x"),
                split_axis=0,
                concat_axis=0,
                tiled=True,
            )
        got = got.reshape((zl, nx) + got.shape[1:])
        partial = spread(got, repeat)
        sums = lax.all_to_all(partial, "narrow", split_axis=0, concat_axis=0, tiled=True)
        if repeat < ITERS - 1:
            packed = call(step_kernel, packed_shape, 3, limit=4 << 20)(sums, hidden, marks)
    return call(last_kernel, shape((nodes, w_out.shape[1]), f32), 4, limit=4 << 20)(
        sums, hidden, w_out, bias_out[None, :]
    )


def solution(mesh):
    wide, narrow = mesh.devices.shape
    nx = 4 if wide % 64 == 0 else 2
    zl = 2
    split_mesh = Mesh(
        mesh.devices.reshape(wide // (zl * nx), zl, nx, narrow), ("zh", "zl", "x", "narrow")
    )
    wide_axes = ("zh", "zl", "x")
    all_axes = wide_axes + ("narrow",)
    in_specs = (
        P(all_axes, None),
        P(wide_axes, "narrow", None, None),
        P(wide_axes, "narrow", None),
        P(all_axes, None),
        P(),
        P(),
        P(),
        P(),
        P(),
        P(wide_axes, "narrow", None, None, None),
        P(wide_axes, "narrow", None),
        P(wide_axes, "narrow", None),
        P(wide_axes, "narrow"),
        P(all_axes),
    )
    return jax.shard_map(
        body, mesh=split_mesh, in_specs=in_specs, out_specs=P(all_axes, None), check_vma=False
    )
```

```python
import functools

import jax
import jax.numpy as jnp
from jax import lax
from jax.experimental import pallas as pl
from jax.experimental.pallas import tpu as pltpu
from jax.sharding import Mesh
from jax.sharding import PartitionSpec as P

ITERS = 3
TELEPORT = 0.1
TOP = 32767.0
TINY = 1e-30
INTERPRET = False

f32 = jnp.float32
bf16 = jnp.bfloat16
i32 = jnp.int32
i16 = jnp.int16


def call(body, out_shape, n_in, scratch=(), in_specs=None, flops=0, nbytes=0, limit=24 << 20):
    vmem = pl.BlockSpec(memory_space=pltpu.VMEM)
    outs = out_shape if isinstance(out_shape, (list, tuple)) else [out_shape]
    return pl.pallas_call(
        body,
        out_shape=out_shape,
        in_specs=in_specs or [vmem] * n_in,
        out_specs=[vmem] * len(outs) if isinstance(out_shape, (list, tuple)) else vmem,
        scratch_shapes=list(scratch),
        compiler_params=pltpu.CompilerParams(vmem_limit_bytes=limit),
        cost_estimate=pl.CostEstimate(flops=flops, bytes_accessed=nbytes, transcendentals=0),
        interpret=INTERPRET,
    )


def dot(a, b, dims=((1,), (0,))):
    return lax.dot_general(a, b, (dims, ((), ())), preferred_element_type=f32)


def split(x):
    hi = x.astype(bf16)
    return hi, (x - hi.astype(f32)).astype(bf16)


def lane_sums(x):
    ones = jnp.ones((8, x.shape[1]), bf16)
    hi, rest = x.astype(bf16), x - x.astype(bf16).astype(f32)
    mid, lo = split(rest)
    over = ((1,), (1,))
    return (dot(ones, lo, over) + dot(ones, mid, over)) + dot(ones, hi, over)


def encode(z, s, dangling, out_ref):
    nodes = z.shape[0]
    top = jnp.max(jnp.abs(z), axis=0, keepdims=True)
    dsum = jnp.sum(z * dangling[:nodes], axis=0, keepdims=True)
    ssum = jnp.sum(s * dangling[nodes : nodes + 1], axis=1, keepdims=True)
    row = lax.broadcasted_iota(i32, (8, z.shape[1]), 0)
    extra = jnp.where((row & 3) == 0, top, 0.0)
    extra = jnp.where((row & 3) == 1, s, extra)
    extra = jnp.where((row & 3) == 2, dsum, extra)
    extra = jnp.where((row & 3) == 3, ssum, extra)
    level = jnp.ceil(jnp.log2(jnp.maximum(jnp.abs(extra), TINY)) * 256.0)
    level = jnp.minimum(level, TOP)
    gain = TOP * jnp.exp2(level * (-1.0 / 256.0))
    codes = jnp.clip(jnp.round(z * gain[0:1]), -TOP, TOP)
    extra_codes = jnp.clip(jnp.round(extra * gain), -TOP, TOP)
    tail = jnp.where(row < 4, level, extra_codes)
    packed = jnp.concatenate([codes, tail], axis=0).astype(i32).astype(i16)
    for k in range(out_ref.shape[0]):
        out_ref[k] = packed


def head_kernel(
    count_hbm,
    send_hbm,
    features_hbm,
    rows_hbm,
    cols_hbm,
    used_hbm,
    tiles_hbm,
    linked_hbm,
    dangling_hbm,
    outgoing_ref,
    panel_ref,
    sums_ref,
    own_ref,
    far_ref,
    marks_ref,
    count_ref,
    send_ref,
    features_ref,
    rows_ref,
    cols_ref,
    used_ref,
    tiles_ref,
    linked_ref,
    dangling_ref,
    turned_ref,
    index_ref,
    total,
    sems,
):
    pairs = (
        (count_hbm, count_ref),
        (send_hbm, send_ref),
        (features_hbm, features_ref),
        (linked_hbm, linked_ref),
        (dangling_hbm, dangling_ref),
        (rows_hbm, rows_ref),
        (cols_hbm, cols_ref),
        (used_hbm, used_ref),
        (tiles_hbm, tiles_ref),
    )
    loads = [pltpu.make_async_copy(a, b, sems.at[k]) for k, (a, b) in enumerate(pairs)]
    for load in loads:
        load.start()

    row_tiles = panel_ref.shape[0] // 256
    col_tiles = panel_ref.shape[1] // 128
    zero = jnp.zeros((128, 128), f32)

    def clear(p, _):
        total[p] = zero
        return 0

    lax.fori_loop(0, row_tiles * col_tiles, clear, 0)
    for load in loads[:5]:
        load.wait()

    features = features_ref[...]
    nodes = features.shape[0]
    capacity, lists = send_ref.shape
    per_row = 128 // capacity
    lane = lax.broadcasted_iota(i32, (1, 128), 1)
    row = lax.broadcasted_iota(i32, (nodes, 128), 0)
    over = ((1,), (1,))
    square = (lists, lists)
    turn = lax.broadcasted_iota(i32, square, 0) == lax.broadcasted_iota(i32, square, 1)
    turned_ref[...] = dot(
        turn.astype(f32).astype(bf16), send_ref[...].astype(f32).astype(bf16), over
    ).astype(i32)
    for m in range(per_row):
        index_ref[:, pl.ds(m * capacity, capacity)] = turned_ref[
            pl.ds(m, lists // per_row, stride=per_row), :
        ]
    for k in range(lists // per_row):
        end = count_ref[0, k * per_row]
        for m in range(1, per_row):
            end = jnp.where(lane >= m * capacity, count_ref[0, k * per_row + m] + m * capacity, end)
        index = jnp.where(lane < end, index_ref[k : k + 1, :], -1)
        chosen = (row == index).astype(f32).astype(bf16)
        outgoing_ref[pl.ds(k * 128, 128), :] = dot(chosen, features, ((0,), (0,))).astype(bf16)

    same = lax.broadcasted_iota(i32, (nodes, nodes), 0) == lax.broadcasted_iota(
        i32, (nodes, nodes), 1
    )
    eye = same.astype(f32).astype(bf16)
    linked = linked_ref[...]
    high = linked >> 6
    linked = 64.0 * dot(eye, high.astype(f32).astype(bf16), over) + dot(
        eye, (linked - (high << 6)).astype(f32).astype(bf16), over
    )
    linked = linked.astype(i32)

    def counts(width, offset):
        slot = lax.broadcasted_iota(i32, (nodes, width), 1) + offset
        got = jnp.zeros((nodes, width), f32)
        for k in range(linked.shape[1]):
            got = got + jnp.where(linked[:, k : k + 1] == slot, 1.0, 0.0)
        return got.astype(bf16)

    own_ref[...] = counts(nodes, 0)
    for c in range(0, far_ref.shape[1], 256):
        far_ref[:, pl.ds(c, 256)] = counts(256, nodes + c)

    mark = dangling_ref[...].astype(f32)
    column = jnp.sum(jnp.where(same, jnp.broadcast_to(mark, same.shape), 0.0), axis=1, keepdims=True)
    marks_ref[pl.ds(0, nodes), :] = jnp.broadcast_to(column, (nodes, 128))
    marks_ref[pl.ds(nodes, 8), :] = jnp.zeros((8, 128), f32)
    marks_ref[pl.ds(nodes, 8), pl.ds(0, nodes)] = jnp.broadcast_to(mark, (8, nodes))

    for load in loads[5:]:
        load.wait()

    def place(t, _):
        p = rows_ref[0, t] * col_tiles + cols_ref[0, t]
        total[p] = total[p] + tiles_ref[t].astype(f32)
        return 0

    lax.fori_loop(0, used_ref[0, 0], place, 0)

    def store(r, _):
        at = pl.ds(pl.multiple_of(r * 128, 128), 128)
        below = pl.ds(pl.multiple_of((r + row_tiles) * 128, 128), 128)
        whole = jnp.zeros((128, 128), f32)
        for c in range(col_tiles):
            tile = total[r * col_tiles + c]
            whole = whole + tile
            panel_ref[at, pl.ds(c * 128, 128)], panel_ref[below, pl.ds(c * 128, 128)] = split(tile)
        sums_ref[:, at] = lane_sums(whole)
        return 0

    lax.fori_loop(0, row_tiles, store, 0)


def hidden_kernel(
    degree,
    features_ref,
    received_ref,
    own_ref,
    far_ref,
    w_self_ref,
    w_neigh_ref,
    bias_ref,
    dangling_ref,
    hidden_ref,
    out_ref,
):
    features = features_ref[...]
    pooled = dot(own_ref[...], features) + dot(far_ref[...], received_ref[...])
    aggregate = (pooled * (1.0 / degree)).astype(bf16)
    hidden = dot(features, w_self_ref[...]) + dot(aggregate, w_neigh_ref[...]) + bias_ref[...]
    hidden = jnp.maximum(hidden, 0.0)
    hidden_ref[...] = hidden
    encode(hidden, jnp.ones((1, hidden.shape[1]), f32), dangling_ref[...], out_ref)


def spread_kernel(node_total, parts, first, panel_ref, sums_ref, packed_ref, out_ref, z_parts, s_row):
    zh, zl, nx = parts
    half = panel_ref.shape[0] // 2
    nodes = 64
    d_all = jnp.zeros((1, 128), f32)
    ds_all = jnp.zeros((1, 128), f32)
    lane = lax.broadcasted_iota(i32, (1, 128), 1)
    before = None
    for a in range(zh * zl * nx):
        h, m, x = a // (zl * nx), (a // nx) % zl, a % nx
        codes = packed_ref[m, x, h].astype(i32).astype(f32)
        tail = codes[nodes:]
        step = jnp.exp2(tail * (1.0 / 256.0)) * (1.0 / TOP)
        hi, lo = split(codes[:nodes] * step[0:1])
        z_parts[pl.ds(a * nodes, nodes), pl.ds(0, 128)] = hi
        z_parts[pl.ds(a * nodes, nodes), pl.ds(128, 128)] = lo
        extra = pltpu.roll(tail, 4, 0) * step
        d_all = d_all + extra[2:3]
        ds_all = ds_all + extra[3:4]
        if a % 2 and not first:
            s_row[0:1, pl.ds((a // 2) * 128, 128)] = jnp.where(lane < nodes, before, extra[1:2])
        before = extra[1:2]
    d_all = d_all * (1.0 / node_total)
    ds_all = ds_all * (1.0 / node_total)
    upper = dot(panel_ref[:half], z_parts[...])
    lower = dot(panel_ref[half:], z_parts[...])
    z_sum = (upper[:, :128] + upper[:, 128:]) + (lower[:, :128] + lower[:, 128:]) + d_all
    if first:
        s_sum = sums_ref[...]
    else:
        part = jnp.zeros((half, 128), f32)
        for c in range(panel_ref.shape[1] // 128):
            at = pl.ds(c * 128, 128)
            tile = panel_ref[:half, at].astype(f32) + panel_ref[half:, at].astype(f32)
            part = part + tile * s_row[0:1, at]
        s_sum = lane_sums(part)
    for b in range(half // nodes):
        out_ref[b, pl.ds(0, nodes), :] = z_sum[b * nodes : (b + 1) * nodes]
        two = s_sum[:, (b // 2) * 128 : (b // 2) * 128 + 128]
        if b % 2:
            two = pltpu.roll(two, nodes, 1)
        out_ref[b, pl.ds(nodes, 8), :] = two + ds_all


def gather_step(received_ref, hidden_ref):
    nodes = hidden_ref.shape[0]
    total = received_ref[0]
    for j in range(1, received_ref.shape[0]):
        total = total + received_ref[j]
    z = (1.0 - TELEPORT) * total[:nodes] + TELEPORT * hidden_ref[...]
    s = (1.0 - TELEPORT) * total[nodes : nodes + 1] + TELEPORT
    return z, s


def step_kernel(received_ref, hidden_ref, dangling_ref, out_ref):
    z, s = gather_step(received_ref, hidden_ref)
    s8 = jnp.broadcast_to(s, (8, 128))
    lane = lax.broadcasted_iota(i32, (8, 128), 1)
    s8 = jnp.where(lane < z.shape[0], s8, pltpu.roll(s8, z.shape[0], 1))
    encode(z, s8[0:1], dangling_ref[...], out_ref)


def last_kernel(received_ref, hidden_ref, w_ref, bias_ref, out_ref):
    z, s = gather_step(received_ref, hidden_ref)
    nodes = z.shape[0]
    hi = z.astype(bf16)
    mid, lo = split(z - hi.astype(f32))
    w = w_ref[...]
    same = lax.broadcasted_iota(i32, (nodes, 128), 0) == lax.broadcasted_iota(i32, (nodes, 128), 1)
    column = jnp.sum(jnp.where(same, jnp.broadcast_to(s, (nodes, 128)), 0.0), axis=1, keepdims=True)
    out_ref[...] = (dot(lo, w) + dot(mid, w)) + dot(hi, w) + column * bias_ref[...]


def body(
    features,
    send_rows,
    send_count,
    neighbors,
    w_self,
    w_neigh,
    bias_hidden,
    w_out,
    bias_out,
    tiles,
    tile_rows,
    tile_cols,
    tile_count,
    dangling,
):
    shape = jax.ShapeDtypeStruct
    nodes, width = features.shape
    zh, zl, nx = (lax.axis_size(name) for name in ("zh", "zl", "x"))
    wide = zh * zl * nx
    narrow = lax.axis_size("narrow")
    capacity = send_rows.shape[-1]
    slots = wide * capacity
    row_total = narrow * nodes
    col_total = wide * nodes
    node_total = row_total * wide
    degree = neighbors.shape[1]

    keep = functools.partial(pltpu.with_memory_space_constraint, memory_space=pltpu.HBM)
    outgoing, panel, row_sums, own, far, marks = call(
        head_kernel,
        [
            shape((slots, width), bf16),
            shape((2 * row_total, col_total), bf16),
            shape((8, row_total), f32),
            shape((nodes, nodes), bf16),
            shape((nodes, slots), bf16),
            shape((nodes + 8, 128), f32),
        ],
        9,
        in_specs=[pl.BlockSpec(memory_space=pltpu.HBM)] * 9,
        scratch=[
            pltpu.SMEM((1, wide), i32),
            pltpu.VMEM((capacity, wide), i32),
            pltpu.VMEM((nodes, width), bf16),
            pltpu.SMEM(tile_rows.shape[1:], i32),
            pltpu.SMEM(tile_rows.shape[1:], i32),
            pltpu.SMEM((1, 1), i32),
            pltpu.VMEM(tiles.shape[2:], bf16),
            pltpu.VMEM((degree, nodes), i32),
            pltpu.VMEM((1, nodes), i32),
            pltpu.VMEM((wide, capacity), i32),
            pltpu.VMEM((wide * capacity // 128, 128), i32),
            pltpu.VMEM((row_total * col_total // (128 * 128), 128, 128), f32),
            pltpu.SemaphoreType.DMA((9,)),
        ],
        flops=1 << 24,
        nbytes=20 << 20,
        limit=16 << 20,
    )(
        keep(send_count[0]),
        keep(send_rows[0, 0].T),
        keep(features),
        keep(tile_rows[0]),
        keep(tile_cols[0]),
        tile_count,
        keep(tiles[0, 0]),
        keep(neighbors.T),
        keep(dangling[None, :]),
    )
    received = lax.all_to_all(
        outgoing.reshape(wide, capacity, width),
        ("zh", "zl", "x"),
        split_axis=0,
        concat_axis=0,
        tiled=True,
    ).reshape(slots, width)

    packed_shape = shape((zh, nodes + 8, width), i16)
    hidden, packed = call(
        functools.partial(hidden_kernel, degree),
        [shape((nodes, width), f32), packed_shape],
        8,
        limit=8 << 20,
    )(features, received, own, far, w_self, w_neigh, bias_hidden[None, :], marks)

    def spread(packed, repeat):
        return call(
            functools.partial(spread_kernel, node_total, (zh, zl, nx), repeat == 0),
            shape((narrow, nodes + 8, width), f32),
            3,
            scratch=[pltpu.VMEM((col_total, 2 * width), bf16), pltpu.VMEM((8, col_total), f32)],
            flops=2 * 2 * row_total * col_total * 256,
            nbytes=10 << 20,
            limit=12 << 20,
        )(panel, row_sums, packed)

    for repeat in range(ITERS):
        got = lax.all_to_all(packed, "zh", split_axis=0, concat_axis=0, tiled=True)
        got = lax.all_to_all(
            jnp.broadcast_to(got[None], (zl * nx,) + got.shape),
            ("zl", "x"),
            split_axis=0,
            concat_axis=0,
            tiled=True,
        )
        got = got.reshape((zl, nx) + got.shape[1:])
        partial = spread(got, repeat)
        sums = lax.all_to_all(partial, "narrow", split_axis=0, concat_axis=0, tiled=True)
        if repeat < ITERS - 1:
            packed = call(step_kernel, packed_shape, 3, limit=4 << 20)(sums, hidden, marks)
    return call(last_kernel, shape((nodes, w_out.shape[1]), f32), 4, limit=4 << 20)(
        sums, hidden, w_out, bias_out[None, :]
    )


def solution(mesh):
    wide, narrow = mesh.devices.shape
    nx = 4 if wide % 64 == 0 else 2
    zl = 2
    split_mesh = Mesh(
        mesh.devices.reshape(wide // (zl * nx), zl, nx, narrow), ("zh", "zl", "x", "narrow")
    )
    wide_axes = ("zh", "zl", "x")
    all_axes = wide_axes + ("narrow",)
    in_specs = (
        P(all_axes, None),
        P(wide_axes, "narrow", None, None),
        P(wide_axes, "narrow", None),
        P(all_axes, None),
        P(),
        P(),
        P(),
        P(),
        P(),
        P(wide_axes, "narrow", None, None, None),
        P(wide_axes, "narrow", None),
        P(wide_axes, "narrow", None),
        P(wide_axes, "narrow"),
        P(all_axes),
    )
    return jax.shard_map(
        body, mesh=split_mesh, in_specs=in_specs, out_specs=P(all_axes, None), check_vma=False
    )
```

```python
import functools

import jax
import jax.numpy as jnp
from jax import lax
from jax.experimental import pallas as pl
from jax.experimental.pallas import tpu as pltpu
from jax.sharding import Mesh
from jax.sharding import PartitionSpec as P

ITERS = 3
TELEPORT = 0.1
TOP = 32767.0
TINY = 1e-30
INTERPRET = False

f32 = jnp.float32
bf16 = jnp.bfloat16
i32 = jnp.int32
i16 = jnp.int16


def call(body, out_shape, n_in, scratch=(), in_specs=None, flops=0, nbytes=0, limit=24 << 20):
    vmem = pl.BlockSpec(memory_space=pltpu.VMEM)
    outs = out_shape if isinstance(out_shape, (list, tuple)) else [out_shape]
    return pl.pallas_call(
        body,
        out_shape=out_shape,
        in_specs=in_specs or [vmem] * n_in,
        out_specs=[vmem] * len(outs) if isinstance(out_shape, (list, tuple)) else vmem,
        scratch_shapes=list(scratch),
        compiler_params=pltpu.CompilerParams(vmem_limit_bytes=limit),
        cost_estimate=pl.CostEstimate(flops=flops, bytes_accessed=nbytes, transcendentals=0),
        interpret=INTERPRET,
    )


def dot(a, b, dims=((1,), (0,))):
    return lax.dot_general(a, b, (dims, ((), ())), preferred_element_type=f32)


def split(x):
    hi = x.astype(bf16)
    return hi, (x - hi.astype(f32)).astype(bf16)


def lane_sums(x):
    ones = jnp.ones((8, x.shape[1]), bf16)
    hi, rest = x.astype(bf16), x - x.astype(bf16).astype(f32)
    mid, lo = split(rest)
    over = ((1,), (1,))
    return (dot(ones, lo, over) + dot(ones, mid, over)) + dot(ones, hi, over)


def encode(z, s, dangling, out_ref):
    nodes = z.shape[0]
    top = jnp.max(jnp.abs(z), axis=0, keepdims=True)
    dsum = jnp.sum(z * dangling[:nodes], axis=0, keepdims=True)
    ssum = jnp.sum(s * dangling[nodes : nodes + 1], axis=1, keepdims=True)
    row = lax.broadcasted_iota(i32, (8, z.shape[1]), 0)
    extra = jnp.where((row & 3) == 0, top, 0.0)
    extra = jnp.where((row & 3) == 1, s, extra)
    extra = jnp.where((row & 3) == 2, dsum, extra)
    extra = jnp.where((row & 3) == 3, ssum, extra)
    level = jnp.ceil(jnp.log2(jnp.maximum(jnp.abs(extra), TINY)) * 256.0)
    level = jnp.minimum(level, TOP)
    gain = TOP * jnp.exp2(level * (-1.0 / 256.0))
    codes = jnp.clip(jnp.round(z * gain[0:1]), -TOP, TOP)
    extra_codes = jnp.clip(jnp.round(extra * gain), -TOP, TOP)
    tail = jnp.where(row < 4, level, extra_codes)
    packed = jnp.concatenate([codes, tail], axis=0).astype(i32).astype(i16)
    for k in range(out_ref.shape[0]):
        out_ref[k] = packed


def head_kernel(
    count_hbm,
    send_hbm,
    features_hbm,
    rows_hbm,
    cols_hbm,
    used_hbm,
    tiles_hbm,
    linked_hbm,
    dangling_hbm,
    outgoing_ref,
    panel_ref,
    total,
    sums_ref,
    own_ref,
    far_ref,
    marks_ref,
    count_ref,
    send_ref,
    features_ref,
    rows_ref,
    cols_ref,
    used_ref,
    tiles_ref,
    linked_ref,
    dangling_ref,
    turned_ref,
    index_ref,
    whole_ref,
    sems,
):
    pairs = (
        (count_hbm, count_ref),
        (send_hbm, send_ref),
        (features_hbm, features_ref),
        (linked_hbm, linked_ref),
        (dangling_hbm, dangling_ref),
        (rows_hbm, rows_ref),
        (cols_hbm, cols_ref),
        (used_hbm, used_ref),
        (tiles_hbm, tiles_ref),
    )
    loads = [pltpu.make_async_copy(a, b, sems.at[k]) for k, (a, b) in enumerate(pairs)]
    for load in loads:
        load.start()

    row_tiles = panel_ref.shape[0] // 256
    col_tiles = panel_ref.shape[1] // 128
    zero = jnp.zeros((128, 128), f32)

    def clear(p, _):
        total[p] = zero
        return 0

    lax.fori_loop(0, row_tiles * col_tiles, clear, 0)
    for load in loads[:5]:
        load.wait()

    features = features_ref[...]
    nodes = features.shape[0]
    capacity, lists = send_ref.shape
    per_row = 128 // capacity
    lane = lax.broadcasted_iota(i32, (1, 128), 1)
    row = lax.broadcasted_iota(i32, (nodes, 128), 0)
    over = ((1,), (1,))
    square = (lists, lists)
    turn = lax.broadcasted_iota(i32, square, 0) == lax.broadcasted_iota(i32, square, 1)
    turned_ref[...] = dot(
        turn.astype(f32).astype(bf16), send_ref[...].astype(f32).astype(bf16), over
    ).astype(i32)
    for m in range(per_row):
        index_ref[:, pl.ds(m * capacity, capacity)] = turned_ref[
            pl.ds(m, lists // per_row, stride=per_row), :
        ]
    for k in range(lists // per_row):
        end = count_ref[0, k * per_row]
        for m in range(1, per_row):
            end = jnp.where(lane >= m * capacity, count_ref[0, k * per_row + m] + m * capacity, end)
        index = jnp.where(lane < end, index_ref[k : k + 1, :], -1)
        chosen = (row == index).astype(f32).astype(bf16)
        outgoing_ref[pl.ds(k * 128, 128), :] = dot(chosen, features, ((0,), (0,))).astype(bf16)

    same = lax.broadcasted_iota(i32, (nodes, nodes), 0) == lax.broadcasted_iota(
        i32, (nodes, nodes), 1
    )
    eye = same.astype(f32).astype(bf16)
    linked = linked_ref[...]
    high = linked >> 6
    linked = 64.0 * dot(eye, high.astype(f32).astype(bf16), over) + dot(
        eye, (linked - (high << 6)).astype(f32).astype(bf16), over
    )
    linked = linked.astype(i32)

    def counts(width, offset):
        slot = lax.broadcasted_iota(i32, (nodes, width), 1) + offset
        got = jnp.zeros((nodes, width), f32)
        for k in range(linked.shape[1]):
            got = got + jnp.where(linked[:, k : k + 1] == slot, 1.0, 0.0)
        return got.astype(bf16)

    own_ref[...] = counts(nodes, 0)
    for c in range(0, far_ref.shape[1], 256):
        far_ref[:, pl.ds(c, 256)] = counts(256, nodes + c)

    mark = dangling_ref[...].astype(f32)
    column = jnp.sum(jnp.where(same, jnp.broadcast_to(mark, same.shape), 0.0), axis=1, keepdims=True)
    marks_ref[pl.ds(0, nodes), :] = jnp.broadcast_to(column, (nodes, 128))
    marks_ref[pl.ds(nodes, 8), :] = jnp.zeros((8, 128), f32)
    marks_ref[pl.ds(nodes, 8), pl.ds(0, nodes)] = jnp.broadcast_to(mark, (8, nodes))

    for load in loads[5:]:
        load.wait()

    def place(t, _):
        p = rows_ref[0, t] * col_tiles + cols_ref[0, t]
        total[p] = total[p] + tiles_ref[t].astype(f32)
        return 0

    lax.fori_loop(0, used_ref[0, 0], place, 0)

    def store(g, _):
        at = pl.ds(pl.multiple_of(g * 16, 16), 16)
        below = pl.ds(pl.multiple_of(g * 16 + row_tiles * 128, 16), 16)
        r = g // 8
        inner = pl.ds(pl.multiple_of((g % 8) * 16, 16), 16)
        whole = jnp.zeros((16, 128), f32)
        for c in range(col_tiles):
            tile = total[r * col_tiles + c, inner, :]
            whole = whole + tile
            panel_ref[at, pl.ds(c * 128, 128)], panel_ref[below, pl.ds(c * 128, 128)] = split(tile)
        whole_ref[at, :] = whole
        return 0

    lax.fori_loop(0, row_tiles * 8, store, 0)
    for r in range(row_tiles):
        sums_ref[:, pl.ds(r * 128, 128)] = lane_sums(whole_ref[pl.ds(r * 128, 128), :])


def hidden_kernel(
    degree,
    features_ref,
    received_ref,
    own_ref,
    far_ref,
    w_self_ref,
    w_neigh_ref,
    bias_ref,
    dangling_ref,
    hidden_ref,
    out_ref,
):
    features = features_ref[...]
    pooled = dot(own_ref[...], features) + dot(far_ref[...], received_ref[...])
    aggregate = (pooled * (1.0 / degree)).astype(bf16)
    hidden = dot(features, w_self_ref[...]) + dot(aggregate, w_neigh_ref[...]) + bias_ref[...]
    hidden = jnp.maximum(hidden, 0.0)
    hidden_ref[...] = hidden
    encode(hidden, jnp.ones((1, hidden.shape[1]), f32), dangling_ref[...], out_ref)


def spread_kernel(
    node_total, parts, first, panel_ref, sums_ref, packed_ref, out_ref, z_parts, s_row
):
    zh, zl, nx = parts
    half = panel_ref.shape[0] // 2
    nodes = 64
    d_all = jnp.zeros((1, 128), f32)
    ds_all = jnp.zeros((1, 128), f32)
    lane = lax.broadcasted_iota(i32, (1, 128), 1)
    before = None
    for a in range(zh * zl * nx):
        h, m, x = a // (zl * nx), (a // nx) % zl, a % nx
        codes = packed_ref[m, x, h].astype(i32).astype(f32)
        tail = codes[nodes:]
        step = jnp.exp2(tail * (1.0 / 256.0)) * (1.0 / TOP)
        hi, lo = split(codes[:nodes] * step[0:1])
        z_parts[pl.ds(a * nodes, nodes), pl.ds(0, 128)] = hi
        z_parts[pl.ds(a * nodes, nodes), pl.ds(128, 128)] = lo
        extra = pltpu.roll(tail, 4, 0) * step
        d_all = d_all + extra[2:3]
        ds_all = ds_all + extra[3:4]
        if a % 2 and not first:
            s_row[0:1, pl.ds((a // 2) * 128, 128)] = jnp.where(lane < nodes, before, extra[1:2])
        before = extra[1:2]
    d_all = d_all * (1.0 / node_total)
    ds_all = ds_all * (1.0 / node_total)
    upper = dot(panel_ref[:half], z_parts[...])
    lower = dot(panel_ref[half:], z_parts[...])
    z_sum = (upper[:, :128] + upper[:, 128:]) + (lower[:, :128] + lower[:, 128:]) + d_all
    if first:
        s_sum = sums_ref[...]
    else:
        col_tiles = panel_ref.shape[1] // 128
        pieces = []
        for r in range(half // 128):
            part = sums_ref[r * col_tiles] * s_row[0:1, pl.ds(0, 128)]
            for c in range(1, col_tiles):
                part = part + sums_ref[r * col_tiles + c] * s_row[0:1, pl.ds(c * 128, 128)]
            pieces.append(lane_sums(part))
        s_sum = jnp.concatenate(pieces, axis=1)
    for b in range(half // nodes):
        out_ref[b, pl.ds(0, nodes), :] = z_sum[b * nodes : (b + 1) * nodes]
        two = s_sum[:, (b // 2) * 128 : (b // 2) * 128 + 128]
        if b % 2:
            two = pltpu.roll(two, nodes, 1)
        out_ref[b, pl.ds(nodes, 8), :] = two + ds_all


def gather_step(received_ref, hidden_ref):
    nodes = hidden_ref.shape[0]
    total = received_ref[0]
    for j in range(1, received_ref.shape[0]):
        total = total + received_ref[j]
    z = (1.0 - TELEPORT) * total[:nodes] + TELEPORT * hidden_ref[...]
    s = (1.0 - TELEPORT) * total[nodes : nodes + 1] + TELEPORT
    return z, s


def step_kernel(received_ref, hidden_ref, dangling_ref, out_ref):
    z, s = gather_step(received_ref, hidden_ref)
    s8 = jnp.broadcast_to(s, (8, 128))
    lane = lax.broadcasted_iota(i32, (8, 128), 1)
    s8 = jnp.where(lane < z.shape[0], s8, pltpu.roll(s8, z.shape[0], 1))
    encode(z, s8[0:1], dangling_ref[...], out_ref)


def last_kernel(received_ref, hidden_ref, w_ref, bias_ref, out_ref):
    z, s = gather_step(received_ref, hidden_ref)
    nodes = z.shape[0]
    hi = z.astype(bf16)
    mid, lo = split(z - hi.astype(f32))
    w = w_ref[...]
    same = lax.broadcasted_iota(i32, (nodes, 128), 0) == lax.broadcasted_iota(i32, (nodes, 128), 1)
    column = jnp.sum(jnp.where(same, jnp.broadcast_to(s, (nodes, 128)), 0.0), axis=1, keepdims=True)
    out_ref[...] = (dot(lo, w) + dot(mid, w)) + dot(hi, w) + column * bias_ref[...]


def body(
    features,
    send_rows,
    send_count,
    neighbors,
    w_self,
    w_neigh,
    bias_hidden,
    w_out,
    bias_out,
    tiles,
    tile_rows,
    tile_cols,
    tile_count,
    dangling,
):
    shape = jax.ShapeDtypeStruct
    nodes, width = features.shape
    zh, zl, nx = (lax.axis_size(name) for name in ("zh", "zl", "x"))
    wide = zh * zl * nx
    narrow = lax.axis_size("narrow")
    capacity = send_rows.shape[-1]
    slots = wide * capacity
    row_total = narrow * nodes
    col_total = wide * nodes
    node_total = row_total * wide
    degree = neighbors.shape[1]

    keep = functools.partial(pltpu.with_memory_space_constraint, memory_space=pltpu.HBM)
    outgoing, panel, total, row_sums, own, far, marks = call(
        head_kernel,
        [
            shape((slots, width), bf16),
            shape((2 * row_total, col_total), bf16),
            shape((row_total * col_total // (128 * 128), 128, 128), f32),
            shape((8, row_total), f32),
            shape((nodes, nodes), bf16),
            shape((nodes, slots), bf16),
            shape((nodes + 8, 128), f32),
        ],
        9,
        in_specs=[pl.BlockSpec(memory_space=pltpu.HBM)] * 9,
        scratch=[
            pltpu.SMEM((1, wide), i32),
            pltpu.VMEM((capacity, wide), i32),
            pltpu.VMEM((nodes, width), bf16),
            pltpu.SMEM(tile_rows.shape[1:], i32),
            pltpu.SMEM(tile_rows.shape[1:], i32),
            pltpu.SMEM((1, 1), i32),
            pltpu.VMEM(tiles.shape[2:], bf16),
            pltpu.VMEM((degree, nodes), i32),
            pltpu.VMEM((1, nodes), i32),
            pltpu.VMEM((wide, capacity), i32),
            pltpu.VMEM((wide * capacity // 128, 128), i32),
            pltpu.VMEM((row_total, 128), f32),
            pltpu.SemaphoreType.DMA((9,)),
        ],
        flops=1 << 24,
        nbytes=20 << 20,
        limit=16 << 20,
    )(
        keep(send_count[0]),
        keep(send_rows[0, 0].T),
        keep(features),
        keep(tile_rows[0]),
        keep(tile_cols[0]),
        tile_count,
        keep(tiles[0, 0]),
        keep(neighbors.T),
        keep(dangling[None, :]),
    )
    received = lax.all_to_all(
        outgoing.reshape(wide, capacity, width),
        ("zh", "zl", "x"),
        split_axis=0,
        concat_axis=0,
        tiled=True,
    ).reshape(slots, width)

    packed_shape = shape((zh, nodes + 8, width), i16)
    hidden, packed = call(
        functools.partial(hidden_kernel, degree),
        [shape((nodes, width), f32), packed_shape],
        8,
        limit=8 << 20,
    )(features, received, own, far, w_self, w_neigh, bias_hidden[None, :], marks)

    def spread(packed, repeat):
        return call(
            functools.partial(spread_kernel, node_total, (zh, zl, nx), repeat == 0),
            shape((narrow, nodes + 8, width), f32),
            3,
            scratch=[pltpu.VMEM((col_total, 2 * width), bf16), pltpu.VMEM((8, col_total), f32)],
            flops=2 * 2 * row_total * col_total * 256,
            nbytes=10 << 20,
            limit=12 << 20,
        )(panel, row_sums if repeat == 0 else total, packed)

    for repeat in range(ITERS):
        got = lax.all_to_all(packed, "zh", split_axis=0, concat_axis=0, tiled=True)
        got = lax.all_to_all(
            jnp.broadcast_to(got[None], (zl * nx,) + got.shape),
            ("zl", "x"),
            split_axis=0,
            concat_axis=0,
            tiled=True,
        )
        got = got.reshape((zl, nx) + got.shape[1:])
        partial = spread(got, repeat)
        sums = lax.all_to_all(partial, "narrow", split_axis=0, concat_axis=0, tiled=True)
        if repeat < ITERS - 1:
            packed = call(step_kernel, packed_shape, 3, limit=4 << 20)(sums, hidden, marks)
    return call(last_kernel, shape((nodes, w_out.shape[1]), f32), 4, limit=4 << 20)(
        sums, hidden, w_out, bias_out[None, :]
    )


def solution(mesh):
    wide, narrow = mesh.devices.shape
    nx = 4 if wide % 64 == 0 else 2
    zl = 2
    split_mesh = Mesh(
        mesh.devices.reshape(wide // (zl * nx), zl, nx, narrow), ("zh", "zl", "x", "narrow")
    )
    wide_axes = ("zh", "zl", "x")
    all_axes = wide_axes + ("narrow",)
    in_specs = (
        P(all_axes, None),
        P(wide_axes, "narrow", None, None),
        P(wide_axes, "narrow", None),
        P(all_axes, None),
        P(),
        P(),
        P(),
        P(),
        P(),
        P(wide_axes, "narrow", None, None, None),
        P(wide_axes, "narrow", None),
        P(wide_axes, "narrow", None),
        P(wide_axes, "narrow"),
        P(all_axes),
    )
    return jax.shard_map(
        body, mesh=split_mesh, in_specs=in_specs, out_specs=P(all_axes, None), check_vma=False
    )
```

```python
import functools

import jax
import jax.numpy as jnp
from jax import lax
from jax.experimental import pallas as pl
from jax.experimental.pallas import tpu as pltpu
from jax.sharding import Mesh
from jax.sharding import PartitionSpec as P

ITERS = 3
TELEPORT = 0.1
TOP = 32767.0
TINY = 1e-30
INTERPRET = False

f32 = jnp.float32
bf16 = jnp.bfloat16
i32 = jnp.int32
i16 = jnp.int16


def call(body, out_shape, n_in, scratch=(), in_specs=None, flops=0, nbytes=0, limit=24 << 20):
    vmem = pl.BlockSpec(memory_space=pltpu.VMEM)
    outs = out_shape if isinstance(out_shape, (list, tuple)) else [out_shape]
    return pl.pallas_call(
        body,
        out_shape=out_shape,
        in_specs=in_specs or [vmem] * n_in,
        out_specs=[vmem] * len(outs) if isinstance(out_shape, (list, tuple)) else vmem,
        scratch_shapes=list(scratch),
        compiler_params=pltpu.CompilerParams(vmem_limit_bytes=limit),
        cost_estimate=pl.CostEstimate(flops=flops, bytes_accessed=nbytes, transcendentals=0),
        interpret=INTERPRET,
    )


def dot(a, b, dims=((1,), (0,))):
    return lax.dot_general(a, b, (dims, ((), ())), preferred_element_type=f32)


def split(x):
    hi = x.astype(bf16)
    return hi, (x - hi.astype(f32)).astype(bf16)


def lane_sums(x):
    ones = jnp.ones((8, x.shape[1]), bf16)
    hi, rest = x.astype(bf16), x - x.astype(bf16).astype(f32)
    mid, lo = split(rest)
    over = ((1,), (1,))
    return (dot(ones, lo, over) + dot(ones, mid, over)) + dot(ones, hi, over)


def encode(z, s, dangling, out_ref):
    nodes = z.shape[0]
    top = jnp.max(jnp.abs(z), axis=0, keepdims=True)
    dsum = jnp.sum(z * dangling[:nodes], axis=0, keepdims=True)
    ssum = jnp.sum(s * dangling[nodes : nodes + 1], axis=1, keepdims=True)
    row = lax.broadcasted_iota(i32, (8, z.shape[1]), 0)
    extra = jnp.where((row & 3) == 0, top, 0.0)
    extra = jnp.where((row & 3) == 1, s, extra)
    extra = jnp.where((row & 3) == 2, dsum, extra)
    extra = jnp.where((row & 3) == 3, ssum, extra)
    level = jnp.ceil(jnp.log2(jnp.maximum(jnp.abs(extra), TINY)) * 256.0)
    level = jnp.minimum(level, TOP)
    gain = TOP * jnp.exp2(level * (-1.0 / 256.0))
    codes = jnp.clip(jnp.round(z * gain[0:1]), -TOP, TOP)
    extra_codes = jnp.clip(jnp.round(extra * gain), -TOP, TOP)
    tail = jnp.where(row < 4, level, extra_codes)
    packed = jnp.concatenate([codes, tail], axis=0).astype(i32).astype(i16)
    for k in range(out_ref.shape[0]):
        out_ref[k] = packed


def head_kernel(
    count_hbm,
    send_hbm,
    features_hbm,
    rows_hbm,
    cols_hbm,
    used_hbm,
    tiles_hbm,
    linked_hbm,
    dangling_hbm,
    outgoing_ref,
    panel_ref,
    total,
    sums_ref,
    own_ref,
    far_ref,
    marks_ref,
    count_ref,
    send_ref,
    features_ref,
    rows_ref,
    cols_ref,
    used_ref,
    tiles_ref,
    linked_ref,
    dangling_ref,
    turned_ref,
    index_ref,
    whole_ref,
    sems,
):
    pairs = (
        (count_hbm, count_ref),
        (send_hbm, send_ref),
        (features_hbm, features_ref),
        (linked_hbm, linked_ref),
        (dangling_hbm, dangling_ref),
        (rows_hbm, rows_ref),
        (cols_hbm, cols_ref),
        (used_hbm, used_ref),
        (tiles_hbm, tiles_ref),
    )
    loads = [pltpu.make_async_copy(a, b, sems.at[k]) for k, (a, b) in enumerate(pairs)]
    for load in loads:
        load.start()

    row_tiles = panel_ref.shape[0] // 256
    col_tiles = panel_ref.shape[1] // 128
    zero = jnp.zeros((128, 128), f32)

    def clear(p, _):
        total[p] = zero
        return 0

    lax.fori_loop(0, row_tiles * col_tiles, clear, 0)
    for load in loads[:5]:
        load.wait()

    features = features_ref[...]
    nodes = features.shape[0]
    capacity, lists = send_ref.shape
    per_row = 128 // capacity
    lane = lax.broadcasted_iota(i32, (1, 128), 1)
    row = lax.broadcasted_iota(i32, (nodes, 128), 0)
    over = ((1,), (1,))
    square = (lists, lists)
    turn = lax.broadcasted_iota(i32, square, 0) == lax.broadcasted_iota(i32, square, 1)
    turned_ref[...] = dot(
        turn.astype(f32).astype(bf16), send_ref[...].astype(f32).astype(bf16), over
    ).astype(i32)
    for m in range(per_row):
        index_ref[:, pl.ds(m * capacity, capacity)] = turned_ref[
            pl.ds(m, lists // per_row, stride=per_row), :
        ]
    for k in range(lists // per_row):
        end = count_ref[0, k * per_row]
        for m in range(1, per_row):
            end = jnp.where(lane >= m * capacity, count_ref[0, k * per_row + m] + m * capacity, end)
        index = jnp.where(lane < end, index_ref[k : k + 1, :], -1)
        chosen = (row == index).astype(f32).astype(bf16)
        outgoing_ref[pl.ds(k * 128, 128), :] = dot(chosen, features, ((0,), (0,))).astype(bf16)

    same = lax.broadcasted_iota(i32, (nodes, nodes), 0) == lax.broadcasted_iota(
        i32, (nodes, nodes), 1
    )
    eye = same.astype(f32).astype(bf16)
    linked = linked_ref[...]
    high = linked >> 6
    linked = 64.0 * dot(eye, high.astype(f32).astype(bf16), over) + dot(
        eye, (linked - (high << 6)).astype(f32).astype(bf16), over
    )
    linked = linked.astype(i32)

    def counts(width, offset):
        slot = lax.broadcasted_iota(i32, (nodes, width), 1) + offset
        got = jnp.zeros((nodes, width), f32)
        for k in range(linked.shape[1]):
            got = got + jnp.where(linked[:, k : k + 1] == slot, 1.0, 0.0)
        return got.astype(bf16)

    own_ref[...] = counts(nodes, 0)
    for c in range(0, far_ref.shape[1], 256):
        far_ref[:, pl.ds(c, 256)] = counts(256, nodes + c)

    mark = dangling_ref[...].astype(f32)
    column = jnp.sum(jnp.where(same, jnp.broadcast_to(mark, same.shape), 0.0), axis=1, keepdims=True)
    marks_ref[pl.ds(0, nodes), :] = jnp.broadcast_to(column, (nodes, 128))
    marks_ref[pl.ds(nodes, 8), :] = jnp.zeros((8, 128), f32)
    marks_ref[pl.ds(nodes, 8), pl.ds(0, nodes)] = jnp.broadcast_to(mark, (8, nodes))

    for load in loads[5:]:
        load.wait()

    def place(t, _):
        p = rows_ref[0, t] * col_tiles + cols_ref[0, t]
        total[p] = total[p] + tiles_ref[t].astype(f32)
        return 0

    lax.fori_loop(0, used_ref[0, 0], place, 0)

    def store(g, _):
        at = pl.ds(pl.multiple_of(g * 16, 16), 16)
        below = pl.ds(pl.multiple_of(g * 16 + row_tiles * 128, 16), 16)
        r = g // 8
        inner = pl.ds(pl.multiple_of((g % 8) * 16, 16), 16)
        whole = jnp.zeros((16, 128), f32)
        for c in range(col_tiles):
            tile = total[r * col_tiles + c, inner, :]
            whole = whole + tile
            panel_ref[at, pl.ds(c * 128, 128)], panel_ref[below, pl.ds(c * 128, 128)] = split(tile)
        whole_ref[at, :] = whole
        return 0

    lax.fori_loop(0, row_tiles * 8, store, 0)
    for r in range(row_tiles):
        sums_ref[:, pl.ds(r * 128, 128)] = lane_sums(whole_ref[pl.ds(r * 128, 128), :])


def hidden_kernel(
    degree,
    features_ref,
    received_ref,
    own_ref,
    far_ref,
    w_self_ref,
    w_neigh_ref,
    bias_ref,
    dangling_ref,
    hidden_ref,
    out_ref,
):
    features = features_ref[...]
    pooled = dot(own_ref[...], features) + dot(far_ref[...], received_ref[...])
    aggregate = (pooled * (1.0 / degree)).astype(bf16)
    hidden = dot(features, w_self_ref[...]) + dot(aggregate, w_neigh_ref[...]) + bias_ref[...]
    hidden = jnp.maximum(hidden, 0.0)
    hidden_ref[...] = hidden
    encode(hidden, jnp.ones((1, hidden.shape[1]), f32), dangling_ref[...], out_ref)


def spread_kernel(
    node_total, parts, first, panel_ref, sums_ref, packed_ref, out_ref, z_parts, s_row
):
    half = panel_ref.shape[0] // 2
    nodes = 64
    d_all = jnp.zeros((1, 128), f32)
    ds_all = jnp.zeros((1, 128), f32)
    lane = lax.broadcasted_iota(i32, (1, 128), 1)
    before = None
    for a, (i, j) in enumerate(parts):
        codes = packed_ref[i, j].astype(i32).astype(f32)
        tail = codes[nodes:]
        step = jnp.exp2(tail * (1.0 / 256.0)) * (1.0 / TOP)
        hi, lo = split(codes[:nodes] * step[0:1])
        z_parts[pl.ds(a * nodes, nodes), pl.ds(0, 128)] = hi
        z_parts[pl.ds(a * nodes, nodes), pl.ds(128, 128)] = lo
        extra = pltpu.roll(tail, 4, 0) * step
        d_all = d_all + extra[2:3]
        ds_all = ds_all + extra[3:4]
        if a % 2 and not first:
            s_row[0:1, pl.ds((a // 2) * 128, 128)] = jnp.where(lane < nodes, before, extra[1:2])
        before = extra[1:2]
    d_all = d_all * (1.0 / node_total)
    ds_all = ds_all * (1.0 / node_total)
    upper = dot(panel_ref[:half], z_parts[...])
    lower = dot(panel_ref[half:], z_parts[...])
    z_sum = (upper[:, :128] + upper[:, 128:]) + (lower[:, :128] + lower[:, 128:]) + d_all
    if first:
        s_sum = sums_ref[...]
    else:
        col_tiles = panel_ref.shape[1] // 128
        pieces = []
        for r in range(half // 128):
            part = sums_ref[r * col_tiles] * s_row[0:1, pl.ds(0, 128)]
            for c in range(1, col_tiles):
                part = part + sums_ref[r * col_tiles + c] * s_row[0:1, pl.ds(c * 128, 128)]
            pieces.append(lane_sums(part))
        s_sum = jnp.concatenate(pieces, axis=1)
    for b in range(half // nodes):
        out_ref[b, pl.ds(0, nodes), :] = z_sum[b * nodes : (b + 1) * nodes]
        two = s_sum[:, (b // 2) * 128 : (b // 2) * 128 + 128]
        if b % 2:
            two = pltpu.roll(two, nodes, 1)
        out_ref[b, pl.ds(nodes, 8), :] = two + ds_all


def gather_step(received_ref, hidden_ref):
    nodes = hidden_ref.shape[0]
    total = received_ref[0]
    for j in range(1, received_ref.shape[0]):
        total = total + received_ref[j]
    z = (1.0 - TELEPORT) * total[:nodes] + TELEPORT * hidden_ref[...]
    s = (1.0 - TELEPORT) * total[nodes : nodes + 1] + TELEPORT
    return z, s


def step_kernel(received_ref, hidden_ref, dangling_ref, out_ref):
    z, s = gather_step(received_ref, hidden_ref)
    s8 = jnp.broadcast_to(s, (8, 128))
    lane = lax.broadcasted_iota(i32, (8, 128), 1)
    s8 = jnp.where(lane < z.shape[0], s8, pltpu.roll(s8, z.shape[0], 1))
    encode(z, s8[0:1], dangling_ref[...], out_ref)


def last_kernel(received_ref, hidden_ref, w_ref, bias_ref, out_ref):
    z, s = gather_step(received_ref, hidden_ref)
    nodes = z.shape[0]
    hi = z.astype(bf16)
    mid, lo = split(z - hi.astype(f32))
    w = w_ref[...]
    same = lax.broadcasted_iota(i32, (nodes, 128), 0) == lax.broadcasted_iota(i32, (nodes, 128), 1)
    column = jnp.sum(jnp.where(same, jnp.broadcast_to(s, (nodes, 128)), 0.0), axis=1, keepdims=True)
    out_ref[...] = (dot(lo, w) + dot(mid, w)) + dot(hi, w) + column * bias_ref[...]


def body(
    features,
    send_rows,
    send_count,
    neighbors,
    w_self,
    w_neigh,
    bias_hidden,
    w_out,
    bias_out,
    tiles,
    tile_rows,
    tile_cols,
    tile_count,
    dangling,
):
    shape = jax.ShapeDtypeStruct
    nodes, width = features.shape
    sizes = {name: lax.axis_size(name) for name in ("zh", "zl", "xh", "xl")}
    wide = sizes["zh"] * sizes["zl"] * sizes["xh"] * sizes["xl"]
    narrow = lax.axis_size("narrow")
    capacity = send_rows.shape[-1]
    slots = wide * capacity
    row_total = narrow * nodes
    col_total = wide * nodes
    node_total = row_total * wide
    degree = neighbors.shape[1]

    keep = functools.partial(pltpu.with_memory_space_constraint, memory_space=pltpu.HBM)
    outgoing, panel, total, row_sums, own, far, marks = call(
        head_kernel,
        [
            shape((slots, width), bf16),
            shape((2 * row_total, col_total), bf16),
            shape((row_total * col_total // (128 * 128), 128, 128), f32),
            shape((8, row_total), f32),
            shape((nodes, nodes), bf16),
            shape((nodes, slots), bf16),
            shape((nodes + 8, 128), f32),
        ],
        9,
        in_specs=[pl.BlockSpec(memory_space=pltpu.HBM)] * 9,
        scratch=[
            pltpu.SMEM((1, wide), i32),
            pltpu.VMEM((capacity, wide), i32),
            pltpu.VMEM((nodes, width), bf16),
            pltpu.SMEM(tile_rows.shape[1:], i32),
            pltpu.SMEM(tile_rows.shape[1:], i32),
            pltpu.SMEM((1, 1), i32),
            pltpu.VMEM(tiles.shape[2:], bf16),
            pltpu.VMEM((degree, nodes), i32),
            pltpu.VMEM((1, nodes), i32),
            pltpu.VMEM((wide, capacity), i32),
            pltpu.VMEM((wide * capacity // 128, 128), i32),
            pltpu.VMEM((row_total, 128), f32),
            pltpu.SemaphoreType.DMA((9,)),
        ],
        flops=1 << 24,
        nbytes=20 << 20,
        limit=16 << 20,
    )(
        keep(send_count[0]),
        keep(send_rows[0, 0].T),
        keep(features),
        keep(tile_rows[0]),
        keep(tile_cols[0]),
        tile_count,
        keep(tiles[0, 0]),
        keep(neighbors.T),
        keep(dangling[None, :]),
    )
    received = lax.all_to_all(
        outgoing.reshape(wide, capacity, width),
        ("zh", "zl", "xh", "xl"),
        split_axis=0,
        concat_axis=0,
        tiled=True,
    ).reshape(slots, width)

    packed_shape = shape((sizes["zh"] * 2, nodes + 8, width), i16)
    hidden, packed = call(
        functools.partial(hidden_kernel, degree),
        [shape((nodes, width), f32), packed_shape],
        8,
        limit=8 << 20,
    )(features, received, own, far, w_self, w_neigh, bias_hidden[None, :], marks)

    def spread(packed, repeat, parts):
        return call(
            functools.partial(spread_kernel, node_total, parts, repeat == 0),
            shape((narrow, nodes + 8, width), f32),
            3,
            scratch=[pltpu.VMEM((col_total, 2 * width), bf16), pltpu.VMEM((8, col_total), f32)],
            flops=2 * 2 * row_total * col_total * 256,
            nbytes=10 << 20,
            limit=12 << 20,
        )(panel, row_sums if repeat == 0 else total, packed)

    def places(one, two):
        found = []
        for a in range(wide):
            at, rest = {}, a
            for name in ("xl", "xh", "zl", "zh"):
                at[name], rest = rest % sizes[name], rest // sizes[name]
            found.append(
                tuple(
                    functools.reduce(lambda n, name: n * sizes[name] + at[name], names, 0)
                    for names in (two, one)
                )
            )
        return tuple(found)

    routes = ((("zh", "zl"), ("xh", "xl")), (("zh", "zl"), ("xh", "xl")), (("zh", "xh"), ("zl", "xl")))
    for repeat in range(ITERS):
        one, two = routes[repeat]
        got = lax.all_to_all(packed, one, split_axis=0, concat_axis=0, tiled=True)
        if repeat == 1:
            got = lax.all_gather(got, two, axis=0)
        else:
            copies = sizes[two[0]] * sizes[two[1]]
            got = lax.all_to_all(
                jnp.broadcast_to(got[None], (copies,) + got.shape),
                two,
                split_axis=0,
                concat_axis=0,
                tiled=True,
            )
        partial = spread(got, repeat, places(one, two))
        sums = lax.all_to_all(partial, "narrow", split_axis=0, concat_axis=0, tiled=True)
        if repeat < ITERS - 1:
            packed = call(step_kernel, packed_shape, 3, limit=4 << 20)(sums, hidden, marks)
    return call(last_kernel, shape((nodes, w_out.shape[1]), f32), 4, limit=4 << 20)(
        sums, hidden, w_out, bias_out[None, :]
    )


def solution(mesh):
    wide, narrow = mesh.devices.shape
    wide_axes = ("zh", "zl", "xh", "xl")
    split_mesh = Mesh(mesh.devices.reshape(wide // 8, 2, 2, 2, narrow), wide_axes + ("narrow",))
    all_axes = wide_axes + ("narrow",)
    in_specs = (
        P(all_axes, None),
        P(wide_axes, "narrow", None, None),
        P(wide_axes, "narrow", None),
        P(all_axes, None),
        P(),
        P(),
        P(),
        P(),
        P(),
        P(wide_axes, "narrow", None, None, None),
        P(wide_axes, "narrow", None),
        P(wide_axes, "narrow", None),
        P(wide_axes, "narrow"),
        P(all_axes),
    )
    return jax.shard_map(
        body, mesh=split_mesh, in_specs=in_specs, out_specs=P(all_axes, None), check_vma=False
    )
```

```python
import functools

import jax
import jax.numpy as jnp
from jax import lax
from jax.experimental import pallas as pl
from jax.experimental.pallas import tpu as pltpu
from jax.sharding import Mesh
from jax.sharding import PartitionSpec as P

ITERS = 3
TELEPORT = 0.1
TOP = 32767.0
TINY = 1e-30
INTERPRET = False

f32 = jnp.float32
bf16 = jnp.bfloat16
i32 = jnp.int32
i16 = jnp.int16


def call(
    body, out_shape, n_in, scratch=(), in_specs=None, flops=0, nbytes=0, limit=24 << 20, away=0
):
    vmem = pl.BlockSpec(memory_space=pltpu.VMEM)
    outs = out_shape if isinstance(out_shape, (list, tuple)) else [out_shape]
    return pl.pallas_call(
        body,
        out_shape=out_shape,
        in_specs=in_specs or [vmem] * n_in,
        out_specs=[pl.BlockSpec(memory_space=pltpu.HBM)] * away + [vmem] * (len(outs) - away)
        if isinstance(out_shape, (list, tuple))
        else vmem,
        scratch_shapes=list(scratch),
        compiler_params=pltpu.CompilerParams(vmem_limit_bytes=limit),
        cost_estimate=pl.CostEstimate(flops=flops, bytes_accessed=nbytes, transcendentals=0),
        interpret=INTERPRET,
    )


def dot(a, b, dims=((1,), (0,))):
    return lax.dot_general(a, b, (dims, ((), ())), preferred_element_type=f32)


def split(x):
    hi = x.astype(bf16)
    return hi, (x - hi.astype(f32)).astype(bf16)


def lane_sums(x):
    ones = jnp.ones((8, x.shape[1]), bf16)
    hi, rest = x.astype(bf16), x - x.astype(bf16).astype(f32)
    mid, lo = split(rest)
    over = ((1,), (1,))
    return (dot(ones, lo, over) + dot(ones, mid, over)) + dot(ones, hi, over)


def encode(z, s, dangling, out_ref):
    nodes = z.shape[0]
    top = jnp.max(jnp.abs(z), axis=0, keepdims=True)
    dsum = jnp.sum(z * dangling[:nodes], axis=0, keepdims=True)
    ssum = jnp.sum(s * dangling[nodes : nodes + 1], axis=1, keepdims=True)
    row = lax.broadcasted_iota(i32, (8, z.shape[1]), 0)
    extra = jnp.where((row & 3) == 0, top, 0.0)
    extra = jnp.where((row & 3) == 1, s, extra)
    extra = jnp.where((row & 3) == 2, dsum, extra)
    extra = jnp.where((row & 3) == 3, ssum, extra)
    level = jnp.ceil(jnp.log2(jnp.maximum(jnp.abs(extra), TINY)) * 256.0)
    level = jnp.minimum(level, TOP)
    gain = TOP * jnp.exp2(level * (-1.0 / 256.0))
    codes = jnp.clip(jnp.round(z * gain[0:1]), -TOP, TOP)
    extra_codes = jnp.clip(jnp.round(extra * gain), -TOP, TOP)
    tail = jnp.where(row < 4, level, extra_codes)
    packed = jnp.concatenate([codes, tail], axis=0).astype(i32).astype(i16)
    for k in range(out_ref.shape[0]):
        out_ref[k] = packed


def pick_kernel(
    count_hbm,
    send_hbm,
    features_hbm,
    outgoing_ref,
    count_ref,
    send_ref,
    features_ref,
    turned_ref,
    index_ref,
    sems,
):
    pairs = ((count_hbm, count_ref), (send_hbm, send_ref), (features_hbm, features_ref))
    loads = [pltpu.make_async_copy(a, b, sems.at[k]) for k, (a, b) in enumerate(pairs)]
    for load in loads:
        load.start()
    for load in loads:
        load.wait()
    features = features_ref[...]
    nodes = features.shape[0]
    capacity, lists = send_ref.shape
    per_row = 128 // capacity
    lane = lax.broadcasted_iota(i32, (1, 128), 1)
    row = lax.broadcasted_iota(i32, (nodes, 128), 0)
    over = ((1,), (1,))
    square = (lists, lists)
    turn = lax.broadcasted_iota(i32, square, 0) == lax.broadcasted_iota(i32, square, 1)
    turned_ref[...] = dot(
        turn.astype(f32).astype(bf16), send_ref[...].astype(f32).astype(bf16), over
    ).astype(i32)
    for m in range(per_row):
        index_ref[:, pl.ds(m * capacity, capacity)] = turned_ref[
            pl.ds(m, lists // per_row, stride=per_row), :
        ]
    for k in range(lists // per_row):
        end = count_ref[0, k * per_row]
        for m in range(1, per_row):
            end = jnp.where(lane >= m * capacity, count_ref[0, k * per_row + m] + m * capacity, end)
        index = jnp.where(lane < end, index_ref[k : k + 1, :], -1)
        chosen = (row == index).astype(f32).astype(bf16)
        outgoing_ref[pl.ds(k * 128, 128), :] = dot(chosen, features, ((0,), (0,))).astype(bf16)


def panel_kernel(
    rows_hbm,
    cols_hbm,
    used_hbm,
    tiles_hbm,
    linked_hbm,
    dangling_hbm,
    panel_hbm,
    total_hbm,
    sums_ref,
    own_ref,
    far_ref,
    marks_ref,
    rows_ref,
    cols_ref,
    used_ref,
    tiles_ref,
    linked_ref,
    dangling_ref,
    whole_ref,
    panel_ref,
    total,
    sems,
):
    pairs = (
        (linked_hbm, linked_ref),
        (dangling_hbm, dangling_ref),
        (rows_hbm, rows_ref),
        (cols_hbm, cols_ref),
        (used_hbm, used_ref),
        (tiles_hbm, tiles_ref),
    )
    loads = [pltpu.make_async_copy(a, b, sems.at[k]) for k, (a, b) in enumerate(pairs)]
    for load in loads:
        load.start()

    nodes = own_ref.shape[0]
    row_tiles = panel_ref.shape[0] // 256
    col_tiles = panel_ref.shape[1] // 128
    zero = jnp.zeros((128, 128), f32)

    def clear(p, _):
        total[p] = zero
        return 0

    lax.fori_loop(0, row_tiles * col_tiles, clear, 0)
    for load in loads[:2]:
        load.wait()

    same = lax.broadcasted_iota(i32, (nodes, nodes), 0) == lax.broadcasted_iota(
        i32, (nodes, nodes), 1
    )
    eye = same.astype(f32).astype(bf16)
    over = ((1,), (1,))
    linked = linked_ref[...]
    high = linked >> 6
    linked = 64.0 * dot(eye, high.astype(f32).astype(bf16), over) + dot(
        eye, (linked - (high << 6)).astype(f32).astype(bf16), over
    )
    linked = linked.astype(i32)

    def counts(width, offset):
        slot = lax.broadcasted_iota(i32, (nodes, width), 1) + offset
        got = jnp.zeros((nodes, width), f32)
        for k in range(linked.shape[1]):
            got = got + jnp.where(linked[:, k : k + 1] == slot, 1.0, 0.0)
        return got.astype(bf16)

    own_ref[...] = counts(nodes, 0)
    for c in range(0, far_ref.shape[1], 256):
        far_ref[:, pl.ds(c, 256)] = counts(256, nodes + c)

    mark = dangling_ref[...].astype(f32)
    column = jnp.sum(jnp.where(same, jnp.broadcast_to(mark, same.shape), 0.0), axis=1, keepdims=True)
    marks_ref[pl.ds(0, nodes), :] = jnp.broadcast_to(column, (nodes, 128))
    marks_ref[pl.ds(nodes, 8), :] = jnp.zeros((8, 128), f32)
    marks_ref[pl.ds(nodes, 8), pl.ds(0, nodes)] = jnp.broadcast_to(mark, (8, nodes))

    for load in loads[2:]:
        load.wait()

    def place(t, _):
        p = rows_ref[0, t] * col_tiles + cols_ref[0, t]
        total[p] = total[p] + tiles_ref[t].astype(f32)
        return 0

    lax.fori_loop(0, used_ref[0, 0], place, 0)

    kept = pltpu.make_async_copy(total, total_hbm, sems.at[6])
    kept.start()

    def store(g, _):
        at = pl.ds(pl.multiple_of(g * 16, 16), 16)
        below = pl.ds(pl.multiple_of(g * 16 + row_tiles * 128, 16), 16)
        r = g // 8
        inner = pl.ds(pl.multiple_of((g % 8) * 16, 16), 16)
        whole = jnp.zeros((16, 128), f32)
        for c in range(col_tiles):
            tile = total[r * col_tiles + c, inner, :]
            whole = whole + tile
            panel_ref[at, pl.ds(c * 128, 128)], panel_ref[below, pl.ds(c * 128, 128)] = split(tile)
        whole_ref[at, :] = whole
        return 0

    lax.fori_loop(0, row_tiles * 8, store, 0)
    for r in range(row_tiles):
        sums_ref[:, pl.ds(r * 128, 128)] = lane_sums(whole_ref[pl.ds(r * 128, 128), :])
    moved = pltpu.make_async_copy(panel_ref, panel_hbm, sems.at[7])
    moved.start()
    kept.wait()
    moved.wait()


def hidden_kernel(
    degree,
    features_ref,
    received_ref,
    own_ref,
    far_ref,
    w_self_ref,
    w_neigh_ref,
    bias_ref,
    dangling_ref,
    hidden_ref,
    out_ref,
):
    features = features_ref[...]
    pooled = dot(own_ref[...], features) + dot(far_ref[...], received_ref[...])
    aggregate = (pooled * (1.0 / degree)).astype(bf16)
    hidden = dot(features, w_self_ref[...]) + dot(aggregate, w_neigh_ref[...]) + bias_ref[...]
    hidden = jnp.maximum(hidden, 0.0)
    hidden_ref[...] = hidden
    encode(hidden, jnp.ones((1, hidden.shape[1]), f32), dangling_ref[...], out_ref)


def first_spread_kernel(
    node_total, parts, panel_hbm, sums_ref, packed_ref, out_ref, panel_ref, z_parts, s_row, sems
):
    piece = panel_ref.shape[0] // 4
    loads = [
        pltpu.make_async_copy(
            panel_hbm.at[pl.ds(k * piece, piece)], panel_ref.at[pl.ds(k * piece, piece)], sems.at[k]
        )
        for k in range(4)
    ]
    for load in loads:
        load.start()
    spread_body(node_total, parts, loads, None, panel_ref, sums_ref, packed_ref, out_ref, z_parts, s_row)


def spread_kernel(
    node_total, parts, panel_ref, total_hbm, packed_ref, out_ref, z_parts, s_row, total, sems
):
    load = pltpu.make_async_copy(total_hbm, total, sems.at[0])
    load.start()
    spread_body(node_total, parts, (), load, panel_ref, total, packed_ref, out_ref, z_parts, s_row)


def spread_body(
    node_total, parts, loads, sums_load, panel_ref, sums_ref, packed_ref, out_ref, z_parts, s_row
):
    first = sums_load is None
    zh, zl, nx = parts
    half = panel_ref.shape[0] // 2
    nodes = 64
    d_all = jnp.zeros((1, 128), f32)
    ds_all = jnp.zeros((1, 128), f32)
    lane = lax.broadcasted_iota(i32, (1, 128), 1)
    before = None
    for a in range(zh * zl * nx):
        h, m, x = a // (zl * nx), (a // nx) % zl, a % nx
        codes = packed_ref[m, x, h].astype(i32).astype(f32)
        tail = codes[nodes:]
        step = jnp.exp2(tail * (1.0 / 256.0)) * (1.0 / TOP)
        hi, lo = split(codes[:nodes] * step[0:1])
        z_parts[pl.ds(a * nodes, nodes), pl.ds(0, 128)] = hi
        z_parts[pl.ds(a * nodes, nodes), pl.ds(128, 128)] = lo
        extra = pltpu.roll(tail, 4, 0) * step
        d_all = d_all + extra[2:3]
        ds_all = ds_all + extra[3:4]
        if a % 2 and not first:
            s_row[0:1, pl.ds((a // 2) * 128, 128)] = jnp.where(lane < nodes, before, extra[1:2])
        before = extra[1:2]
    d_all = d_all * (1.0 / node_total)
    ds_all = ds_all * (1.0 / node_total)
    if first:
        piece = half // 2
        done = []
        for k, load in enumerate(loads):
            load.wait()
            done.append(dot(panel_ref[pl.ds(k * piece, piece), :], z_parts[...]))
        upper = jnp.concatenate(done[:2], axis=0)
        lower = jnp.concatenate(done[2:], axis=0)
    else:
        upper = dot(panel_ref[:half], z_parts[...])
        lower = dot(panel_ref[half:], z_parts[...])
        sums_load.wait()
    z_sum = (upper[:, :128] + upper[:, 128:]) + (lower[:, :128] + lower[:, 128:]) + d_all
    if first:
        s_sum = sums_ref[...]
    else:
        col_tiles = panel_ref.shape[1] // 128
        pieces = []
        for r in range(half // 128):
            part = sums_ref[r * col_tiles] * s_row[0:1, pl.ds(0, 128)]
            for c in range(1, col_tiles):
                part = part + sums_ref[r * col_tiles + c] * s_row[0:1, pl.ds(c * 128, 128)]
            pieces.append(lane_sums(part))
        s_sum = jnp.concatenate(pieces, axis=1)
    for b in range(half // nodes):
        out_ref[b, pl.ds(0, nodes), :] = z_sum[b * nodes : (b + 1) * nodes]
        two = s_sum[:, (b // 2) * 128 : (b // 2) * 128 + 128]
        if b % 2:
            two = pltpu.roll(two, nodes, 1)
        out_ref[b, pl.ds(nodes, 8), :] = two + ds_all


def gather_step(received_ref, hidden_ref):
    nodes = hidden_ref.shape[0]
    total = received_ref[0]
    for j in range(1, received_ref.shape[0]):
        total = total + received_ref[j]
    z = (1.0 - TELEPORT) * total[:nodes] + TELEPORT * hidden_ref[...]
    s = (1.0 - TELEPORT) * total[nodes : nodes + 1] + TELEPORT
    return z, s


def step_kernel(received_ref, hidden_ref, dangling_ref, out_ref):
    z, s = gather_step(received_ref, hidden_ref)
    s8 = jnp.broadcast_to(s, (8, 128))
    lane = lax.broadcasted_iota(i32, (8, 128), 1)
    s8 = jnp.where(lane < z.shape[0], s8, pltpu.roll(s8, z.shape[0], 1))
    encode(z, s8[0:1], dangling_ref[...], out_ref)


def last_kernel(received_ref, hidden_ref, w_ref, bias_ref, out_ref):
    z, s = gather_step(received_ref, hidden_ref)
    nodes = z.shape[0]
    hi = z.astype(bf16)
    mid, lo = split(z - hi.astype(f32))
    w = w_ref[...]
    same = lax.broadcasted_iota(i32, (nodes, 128), 0) == lax.broadcasted_iota(i32, (nodes, 128), 1)
    column = jnp.sum(jnp.where(same, jnp.broadcast_to(s, (nodes, 128)), 0.0), axis=1, keepdims=True)
    out_ref[...] = (dot(lo, w) + dot(mid, w)) + dot(hi, w) + column * bias_ref[...]


def body(
    features,
    send_rows,
    send_count,
    neighbors,
    w_self,
    w_neigh,
    bias_hidden,
    w_out,
    bias_out,
    tiles,
    tile_rows,
    tile_cols,
    tile_count,
    dangling,
):
    shape = jax.ShapeDtypeStruct
    nodes, width = features.shape
    zh, zl, nx = (lax.axis_size(name) for name in ("zh", "zl", "x"))
    wide = zh * zl * nx
    narrow = lax.axis_size("narrow")
    capacity = send_rows.shape[-1]
    slots = wide * capacity
    row_total = narrow * nodes
    col_total = wide * nodes
    node_total = row_total * wide
    degree = neighbors.shape[1]

    keep = functools.partial(pltpu.with_memory_space_constraint, memory_space=pltpu.HBM)
    hbm = pl.BlockSpec(memory_space=pltpu.HBM)
    vmem = pl.BlockSpec(memory_space=pltpu.VMEM)
    panel_shape = (2 * row_total, col_total)
    total_shape = (row_total * col_total // (128 * 128), 128, 128)
    outgoing = call(
        pick_kernel,
        shape((slots, width), bf16),
        3,
        in_specs=[hbm] * 3,
        scratch=[
            pltpu.SMEM((1, wide), i32),
            pltpu.VMEM((capacity, wide), i32),
            pltpu.VMEM((nodes, width), bf16),
            pltpu.VMEM((wide, capacity), i32),
            pltpu.VMEM((wide * capacity // 128, 128), i32),
            pltpu.SemaphoreType.DMA((3,)),
        ],
        limit=4 << 20,
    )(keep(send_count[0]), keep(send_rows[0, 0].T), keep(features))
    panel, total, row_sums, own, far, marks = call(
        panel_kernel,
        [
            pltpu.HBM(panel_shape, bf16),
            pltpu.HBM(total_shape, f32),
            shape((8, row_total), f32),
            shape((nodes, nodes), bf16),
            shape((nodes, slots), bf16),
            shape((nodes + 8, 128), f32),
        ],
        6,
        in_specs=[hbm] * 6,
        away=2,
        scratch=[
            pltpu.SMEM(tile_rows.shape[1:], i32),
            pltpu.SMEM(tile_rows.shape[1:], i32),
            pltpu.SMEM((1, 1), i32),
            pltpu.VMEM(tiles.shape[2:], bf16),
            pltpu.VMEM((degree, nodes), i32),
            pltpu.VMEM((1, nodes), i32),
            pltpu.VMEM((row_total, 128), f32),
            pltpu.VMEM(panel_shape, bf16),
            pltpu.VMEM(total_shape, f32),
            pltpu.SemaphoreType.DMA((8,)),
        ],
        flops=1 << 24,
        nbytes=20 << 20,
        limit=24 << 20,
    )(
        keep(tile_rows[0]),
        keep(tile_cols[0]),
        tile_count,
        keep(tiles[0, 0]),
        keep(neighbors.T),
        keep(dangling[None, :]),
    )
    received = lax.all_to_all(
        outgoing.reshape(wide, capacity, width),
        ("zh", "zl", "x"),
        split_axis=0,
        concat_axis=0,
        tiled=True,
    ).reshape(slots, width)

    packed_shape = shape((zh, nodes + 8, width), i16)
    hidden, packed = call(
        functools.partial(hidden_kernel, degree),
        [shape((nodes, width), f32), packed_shape],
        8,
        limit=8 << 20,
    )(features, received, own, far, w_self, w_neigh, bias_hidden[None, :], marks)

    partial_shape = shape((narrow, nodes + 8, width), f32)
    z_scratch = [pltpu.VMEM((col_total, 2 * width), bf16), pltpu.VMEM((8, col_total), f32)]
    cost = dict(flops=2 * 2 * row_total * col_total * 256, nbytes=10 << 20)
    first_spread = call(
        functools.partial(first_spread_kernel, node_total, (zh, zl, nx)),
        [partial_shape, shape(panel_shape, bf16)],
        3,
        in_specs=[hbm, vmem, vmem],
        scratch=z_scratch + [pltpu.SemaphoreType.DMA((4,))],
        limit=16 << 20,
        **cost,
    )
    spread = call(
        functools.partial(spread_kernel, node_total, (zh, zl, nx)),
        partial_shape,
        3,
        in_specs=[vmem, hbm, vmem],
        scratch=z_scratch + [pltpu.VMEM(total_shape, f32), pltpu.SemaphoreType.DMA((1,))],
        limit=20 << 20,
        **cost,
    )
    for repeat in range(ITERS):
        got = lax.all_to_all(packed, "zh", split_axis=0, concat_axis=0, tiled=True)
        got = lax.all_to_all(
            jnp.broadcast_to(got[None], (zl * nx,) + got.shape),
            ("zl", "x"),
            split_axis=0,
            concat_axis=0,
            tiled=True,
        )
        got = got.reshape((zl, nx) + got.shape[1:])
        if repeat == 0:
            partial, near = first_spread(keep(panel), row_sums, got)
        else:
            partial = spread(near, keep(total), got)
        sums = lax.all_to_all(partial, "narrow", split_axis=0, concat_axis=0, tiled=True)
        if repeat < ITERS - 1:
            packed = call(step_kernel, packed_shape, 3, limit=4 << 20)(sums, hidden, marks)
    return call(last_kernel, shape((nodes, w_out.shape[1]), f32), 4, limit=4 << 20)(
        sums, hidden, w_out, bias_out[None, :]
    )


def solution(mesh):
    wide, narrow = mesh.devices.shape
    nx = 4 if wide % 64 == 0 else 2
    zl = 2
    split_mesh = Mesh(
        mesh.devices.reshape(wide // (zl * nx), zl, nx, narrow), ("zh", "zl", "x", "narrow")
    )
    wide_axes = ("zh", "zl", "x")
    all_axes = wide_axes + ("narrow",)
    in_specs = (
        P(all_axes, None),
        P(wide_axes, "narrow", None, None),
        P(wide_axes, "narrow", None),
        P(all_axes, None),
        P(),
        P(),
        P(),
        P(),
        P(),
        P(wide_axes, "narrow", None, None, None),
        P(wide_axes, "narrow", None),
        P(wide_axes, "narrow", None),
        P(wide_axes, "narrow"),
        P(all_axes),
    )
    return jax.shard_map(
        body, mesh=split_mesh, in_specs=in_specs, out_specs=P(all_axes, None), check_vma=False
    )
```

```python
import functools

import jax
import jax.numpy as jnp
from jax import lax
from jax.experimental import pallas as pl
from jax.experimental.pallas import tpu as pltpu
from jax.sharding import Mesh
from jax.sharding import PartitionSpec as P

ITERS = 3
TELEPORT = 0.1
TOP = 32767.0
TINY = 1e-30
INTERPRET = False

f32 = jnp.float32
bf16 = jnp.bfloat16
i32 = jnp.int32
i16 = jnp.int16


def call(body, out_shape, n_in, scratch=(), in_specs=None, flops=0, nbytes=0, limit=24 << 20):
    vmem = pl.BlockSpec(memory_space=pltpu.VMEM)
    outs = out_shape if isinstance(out_shape, (list, tuple)) else [out_shape]
    return pl.pallas_call(
        body,
        out_shape=out_shape,
        in_specs=in_specs or [vmem] * n_in,
        out_specs=[vmem] * len(outs) if isinstance(out_shape, (list, tuple)) else vmem,
        scratch_shapes=list(scratch),
        compiler_params=pltpu.CompilerParams(vmem_limit_bytes=limit),
        cost_estimate=pl.CostEstimate(flops=flops, bytes_accessed=nbytes, transcendentals=0),
        interpret=INTERPRET,
    )


def dot(a, b, dims=((1,), (0,))):
    return lax.dot_general(a, b, (dims, ((), ())), preferred_element_type=f32)


def split(x):
    hi = x.astype(bf16)
    return hi, (x - hi.astype(f32)).astype(bf16)


def lane_sums(x):
    ones = jnp.ones((8, x.shape[1]), bf16)
    hi, rest = x.astype(bf16), x - x.astype(bf16).astype(f32)
    mid, lo = split(rest)
    over = ((1,), (1,))
    return (dot(ones, lo, over) + dot(ones, mid, over)) + dot(ones, hi, over)


def encode(z, s, dangling, out_ref):
    nodes = z.shape[0]
    top = jnp.max(jnp.abs(z), axis=0, keepdims=True)
    dsum = jnp.sum(z * dangling[:nodes], axis=0, keepdims=True)
    ssum = jnp.sum(s * dangling[nodes : nodes + 1], axis=1, keepdims=True)
    row = lax.broadcasted_iota(i32, (8, z.shape[1]), 0)
    extra = jnp.where((row & 3) == 0, top, 0.0)
    extra = jnp.where((row & 3) == 1, s, extra)
    extra = jnp.where((row & 3) == 2, dsum, extra)
    extra = jnp.where((row & 3) == 3, ssum, extra)
    level = jnp.ceil(jnp.log2(jnp.maximum(jnp.abs(extra), TINY)) * 256.0)
    level = jnp.minimum(level, TOP)
    gain = TOP * jnp.exp2(level * (-1.0 / 256.0))
    codes = jnp.clip(jnp.round(z * gain[0:1]), -TOP, TOP)
    extra_codes = jnp.clip(jnp.round(extra * gain), -TOP, TOP)
    tail = jnp.where(row < 4, level, extra_codes)
    packed = jnp.concatenate([codes, tail], axis=0).astype(i32).astype(i16)
    for k in range(out_ref.shape[0]):
        out_ref[k] = packed


def head_kernel(
    count_hbm,
    send_hbm,
    features_hbm,
    rows_hbm,
    cols_hbm,
    used_hbm,
    tiles_hbm,
    linked_hbm,
    dangling_hbm,
    outgoing_ref,
    panel_ref,
    total,
    sums_ref,
    own_ref,
    far_ref,
    marks_ref,
    count_ref,
    send_ref,
    features_ref,
    rows_ref,
    cols_ref,
    used_ref,
    tiles_ref,
    linked_ref,
    dangling_ref,
    turned_ref,
    index_ref,
    whole_ref,
    sems,
):
    pairs = (
        (count_hbm, count_ref),
        (send_hbm, send_ref),
        (features_hbm, features_ref),
        (linked_hbm, linked_ref),
        (dangling_hbm, dangling_ref),
        (rows_hbm, rows_ref),
        (cols_hbm, cols_ref),
        (used_hbm, used_ref),
        (tiles_hbm, tiles_ref),
    )
    loads = [pltpu.make_async_copy(a, b, sems.at[k]) for k, (a, b) in enumerate(pairs)]
    for load in loads:
        load.start()

    row_tiles = panel_ref.shape[0] // 256
    col_tiles = panel_ref.shape[1] // 128
    zero = jnp.zeros((128, 128), f32)

    def clear(p, _):
        total[p] = zero
        return 0

    lax.fori_loop(0, row_tiles * col_tiles, clear, 0)
    for load in loads[:5]:
        load.wait()

    features = features_ref[...]
    nodes = features.shape[0]
    capacity, lists = send_ref.shape
    per_row = 128 // capacity
    lane = lax.broadcasted_iota(i32, (1, 128), 1)
    row = lax.broadcasted_iota(i32, (nodes, 128), 0)
    over = ((1,), (1,))
    square = (lists, lists)
    turn = lax.broadcasted_iota(i32, square, 0) == lax.broadcasted_iota(i32, square, 1)
    turned_ref[...] = dot(
        turn.astype(f32).astype(bf16), send_ref[...].astype(f32).astype(bf16), over
    ).astype(i32)
    for m in range(per_row):
        index_ref[:, pl.ds(m * capacity, capacity)] = turned_ref[
            pl.ds(m, lists // per_row, stride=per_row), :
        ]
    for k in range(lists // per_row):
        end = count_ref[0, k * per_row]
        for m in range(1, per_row):
            end = jnp.where(lane >= m * capacity, count_ref[0, k * per_row + m] + m * capacity, end)
        index = jnp.where(lane < end, index_ref[k : k + 1, :], -1)
        chosen = (row == index).astype(f32).astype(bf16)
        outgoing_ref[pl.ds(k * 128, 128), :] = dot(chosen, features, ((0,), (0,))).astype(bf16)

    same = lax.broadcasted_iota(i32, (nodes, nodes), 0) == lax.broadcasted_iota(
        i32, (nodes, nodes), 1
    )
    eye = same.astype(f32).astype(bf16)
    linked = linked_ref[...]
    high = linked >> 6
    linked = 64.0 * dot(eye, high.astype(f32).astype(bf16), over) + dot(
        eye, (linked - (high << 6)).astype(f32).astype(bf16), over
    )
    linked = linked.astype(i32)

    def counts(width, offset):
        slot = lax.broadcasted_iota(i32, (nodes, width), 1) + offset
        got = jnp.zeros((nodes, width), f32)
        for k in range(linked.shape[1]):
            got = got + jnp.where(linked[:, k : k + 1] == slot, 1.0, 0.0)
        return got.astype(bf16)

    own_ref[...] = counts(nodes, 0)
    for c in range(0, far_ref.shape[1], 256):
        far_ref[:, pl.ds(c, 256)] = counts(256, nodes + c)

    mark = dangling_ref[...].astype(f32)
    column = jnp.sum(jnp.where(same, jnp.broadcast_to(mark, same.shape), 0.0), axis=1, keepdims=True)
    marks_ref[pl.ds(0, nodes), :] = jnp.broadcast_to(column, (nodes, 128))
    marks_ref[pl.ds(nodes, 8), :] = jnp.zeros((8, 128), f32)
    marks_ref[pl.ds(nodes, 8), pl.ds(0, nodes)] = jnp.broadcast_to(mark, (8, nodes))

    for load in loads[5:]:
        load.wait()

    def place(t, _):
        p = rows_ref[0, t] * col_tiles + cols_ref[0, t]
        total[p] = total[p] + tiles_ref[t].astype(f32)
        return 0

    lax.fori_loop(0, used_ref[0, 0], place, 0)

    def store(g, _):
        at = pl.ds(pl.multiple_of(g * 16, 16), 16)
        below = pl.ds(pl.multiple_of(g * 16 + row_tiles * 128, 16), 16)
        r = g // 8
        inner = pl.ds(pl.multiple_of((g % 8) * 16, 16), 16)
        whole = jnp.zeros((16, 128), f32)
        for c in range(col_tiles):
            tile = total[r * col_tiles + c, inner, :]
            whole = whole + tile
            panel_ref[at, pl.ds(c * 128, 128)], panel_ref[below, pl.ds(c * 128, 128)] = split(tile)
        whole_ref[at, :] = whole
        return 0

    lax.fori_loop(0, row_tiles * 8, store, 0)
    for r in range(row_tiles):
        sums_ref[:, pl.ds(r * 128, 128)] = lane_sums(whole_ref[pl.ds(r * 128, 128), :])


def hidden_kernel(
    degree,
    features_ref,
    received_ref,
    own_ref,
    far_ref,
    w_self_ref,
    w_neigh_ref,
    bias_ref,
    dangling_ref,
    hidden_ref,
    out_ref,
):
    features = features_ref[...]
    pooled = dot(own_ref[...], features) + dot(far_ref[...], received_ref[...])
    aggregate = (pooled * (1.0 / degree)).astype(bf16)
    hidden = dot(features, w_self_ref[...]) + dot(aggregate, w_neigh_ref[...]) + bias_ref[...]
    hidden = jnp.maximum(hidden, 0.0)
    hidden_ref[...] = hidden
    encode(hidden, jnp.ones((1, hidden.shape[1]), f32), dangling_ref[...], out_ref)


def spread_kernel(
    node_total, parts, first, panel_ref, sums_ref, packed_ref, out_ref, z_parts, s_row
):
    zh, zl, nx = parts
    half = panel_ref.shape[0] // 2
    nodes = 64
    d_all = jnp.zeros((1, 128), f32)
    ds_all = jnp.zeros((1, 128), f32)
    lane = lax.broadcasted_iota(i32, (1, 128), 1)
    before = None
    for a in range(zh * zl * nx):
        h, m, x = a // (zl * nx), (a // nx) % zl, a % nx
        codes = packed_ref[x, m, h].astype(i32).astype(f32)
        tail = codes[nodes:]
        step = jnp.exp2(tail * (1.0 / 256.0)) * (1.0 / TOP)
        hi, lo = split(codes[:nodes] * step[0:1])
        z_parts[pl.ds(a * nodes, nodes), pl.ds(0, 128)] = hi
        z_parts[pl.ds(a * nodes, nodes), pl.ds(128, 128)] = lo
        extra = pltpu.roll(tail, 4, 0) * step
        d_all = d_all + extra[2:3]
        ds_all = ds_all + extra[3:4]
        if a % 2 and not first:
            s_row[0:1, pl.ds((a // 2) * 128, 128)] = jnp.where(lane < nodes, before, extra[1:2])
        before = extra[1:2]
    d_all = d_all * (1.0 / node_total)
    ds_all = ds_all * (1.0 / node_total)
    upper = dot(panel_ref[:half], z_parts[...])
    lower = dot(panel_ref[half:], z_parts[...])
    z_sum = (upper[:, :128] + upper[:, 128:]) + (lower[:, :128] + lower[:, 128:]) + d_all
    if first:
        s_sum = sums_ref[...]
    else:
        col_tiles = panel_ref.shape[1] // 128
        pieces = []
        for r in range(half // 128):
            part = sums_ref[r * col_tiles] * s_row[0:1, pl.ds(0, 128)]
            for c in range(1, col_tiles):
                part = part + sums_ref[r * col_tiles + c] * s_row[0:1, pl.ds(c * 128, 128)]
            pieces.append(lane_sums(part))
        s_sum = jnp.concatenate(pieces, axis=1)
    for b in range(half // nodes):
        out_ref[b, pl.ds(0, nodes), :] = z_sum[b * nodes : (b + 1) * nodes]
        two = s_sum[:, (b // 2) * 128 : (b // 2) * 128 + 128]
        if b % 2:
            two = pltpu.roll(two, nodes, 1)
        out_ref[b, pl.ds(nodes, 8), :] = two + ds_all


def gather_step(received_ref, hidden_ref):
    nodes = hidden_ref.shape[0]
    total = received_ref[0]
    for j in range(1, received_ref.shape[0]):
        total = total + received_ref[j]
    z = (1.0 - TELEPORT) * total[:nodes] + TELEPORT * hidden_ref[...]
    s = (1.0 - TELEPORT) * total[nodes : nodes + 1] + TELEPORT
    return z, s


def step_kernel(received_ref, hidden_ref, dangling_ref, out_ref):
    z, s = gather_step(received_ref, hidden_ref)
    s8 = jnp.broadcast_to(s, (8, 128))
    lane = lax.broadcasted_iota(i32, (8, 128), 1)
    s8 = jnp.where(lane < z.shape[0], s8, pltpu.roll(s8, z.shape[0], 1))
    encode(z, s8[0:1], dangling_ref[...], out_ref)


def last_kernel(received_ref, hidden_ref, w_ref, bias_ref, out_ref):
    z, s = gather_step(received_ref, hidden_ref)
    nodes = z.shape[0]
    hi = z.astype(bf16)
    mid, lo = split(z - hi.astype(f32))
    w = w_ref[...]
    same = lax.broadcasted_iota(i32, (nodes, 128), 0) == lax.broadcasted_iota(i32, (nodes, 128), 1)
    column = jnp.sum(jnp.where(same, jnp.broadcast_to(s, (nodes, 128)), 0.0), axis=1, keepdims=True)
    out_ref[...] = (dot(lo, w) + dot(mid, w)) + dot(hi, w) + column * bias_ref[...]


def body(
    features,
    send_rows,
    send_count,
    neighbors,
    w_self,
    w_neigh,
    bias_hidden,
    w_out,
    bias_out,
    tiles,
    tile_rows,
    tile_cols,
    tile_count,
    dangling,
):
    shape = jax.ShapeDtypeStruct
    nodes, width = features.shape
    zh, zl, nx = (lax.axis_size(name) for name in ("zh", "zl", "x"))
    wide = zh * zl * nx
    narrow = lax.axis_size("narrow")
    capacity = send_rows.shape[-1]
    slots = wide * capacity
    row_total = narrow * nodes
    col_total = wide * nodes
    node_total = row_total * wide
    degree = neighbors.shape[1]

    keep = functools.partial(pltpu.with_memory_space_constraint, memory_space=pltpu.HBM)
    outgoing, panel, total, row_sums, own, far, marks = call(
        head_kernel,
        [
            shape((slots, width), bf16),
            shape((2 * row_total, col_total), bf16),
            shape((row_total * col_total // (128 * 128), 128, 128), f32),
            shape((8, row_total), f32),
            shape((nodes, nodes), bf16),
            shape((nodes, slots), bf16),
            shape((nodes + 8, 128), f32),
        ],
        9,
        in_specs=[pl.BlockSpec(memory_space=pltpu.HBM)] * 9,
        scratch=[
            pltpu.SMEM((1, wide), i32),
            pltpu.VMEM((capacity, wide), i32),
            pltpu.VMEM((nodes, width), bf16),
            pltpu.SMEM(tile_rows.shape[1:], i32),
            pltpu.SMEM(tile_rows.shape[1:], i32),
            pltpu.SMEM((1, 1), i32),
            pltpu.VMEM(tiles.shape[2:], bf16),
            pltpu.VMEM((degree, nodes), i32),
            pltpu.VMEM((1, nodes), i32),
            pltpu.VMEM((wide, capacity), i32),
            pltpu.VMEM((wide * capacity // 128, 128), i32),
            pltpu.VMEM((row_total, 128), f32),
            pltpu.SemaphoreType.DMA((9,)),
        ],
        flops=1 << 24,
        nbytes=20 << 20,
        limit=16 << 20,
    )(
        keep(send_count[0]),
        keep(send_rows[0, 0].T),
        keep(features),
        keep(tile_rows[0]),
        keep(tile_cols[0]),
        tile_count,
        keep(tiles[0, 0]),
        keep(neighbors.T),
        keep(dangling[None, :]),
    )
    received = lax.all_to_all(
        outgoing.reshape(wide, capacity, width),
        ("zh", "zl", "x"),
        split_axis=0,
        concat_axis=0,
        tiled=True,
    ).reshape(slots, width)

    packed_shape = shape((zh, nodes + 8, width), i16)
    hidden, packed = call(
        functools.partial(hidden_kernel, degree),
        [shape((nodes, width), f32), packed_shape],
        8,
        limit=8 << 20,
    )(features, received, own, far, w_self, w_neigh, bias_hidden[None, :], marks)

    def spread(packed, repeat):
        return call(
            functools.partial(spread_kernel, node_total, (zh, zl, nx), repeat == 0),
            shape((narrow, nodes + 8, width), f32),
            3,
            scratch=[pltpu.VMEM((col_total, 2 * width), bf16), pltpu.VMEM((8, col_total), f32)],
            flops=2 * 2 * row_total * col_total * 256,
            nbytes=10 << 20,
            limit=12 << 20,
        )(panel, row_sums if repeat == 0 else total, packed)

    for repeat in range(ITERS):
        got = lax.all_to_all(packed, "zh", split_axis=0, concat_axis=0, tiled=True)
        got = lax.all_to_all(
            jnp.broadcast_to(got[None], (zl * nx,) + got.shape),
            ("x", "zl"),
            split_axis=0,
            concat_axis=0,
            tiled=True,
        )
        got = got.reshape((nx, zl) + got.shape[1:])
        partial = spread(got, repeat)
        sums = lax.all_to_all(partial, "narrow", split_axis=0, concat_axis=0, tiled=True)
        if repeat < ITERS - 1:
            packed = call(step_kernel, packed_shape, 3, limit=4 << 20)(sums, hidden, marks)
    return call(last_kernel, shape((nodes, w_out.shape[1]), f32), 4, limit=4 << 20)(
        sums, hidden, w_out, bias_out[None, :]
    )


def solution(mesh):
    wide, narrow = mesh.devices.shape
    nx = 4 if wide % 64 == 0 else 2
    zl = 2
    split_mesh = Mesh(
        mesh.devices.reshape(wide // (zl * nx), zl, nx, narrow), ("zh", "zl", "x", "narrow")
    )
    wide_axes = ("zh", "zl", "x")
    all_axes = wide_axes + ("narrow",)
    in_specs = (
        P(all_axes, None),
        P(wide_axes, "narrow", None, None),
        P(wide_axes, "narrow", None),
        P(all_axes, None),
        P(),
        P(),
        P(),
        P(),
        P(),
        P(wide_axes, "narrow", None, None, None),
        P(wide_axes, "narrow", None),
        P(wide_axes, "narrow", None),
        P(wide_axes, "narrow"),
        P(all_axes),
    )
    return jax.shard_map(
        body, mesh=split_mesh, in_specs=in_specs, out_specs=P(all_axes, None), check_vma=False
    )
```
